256 devices in a mesh: gx: 4 (over z_hi), gy: 4 (over x), ha: 16 (over z_lo, y, core).
Axes of the slice: x: 4, y: 4, z: 8 (z_hi: 4, z_lo: 2; z = z_hi * 2 + z_lo), core: 2. Of those that a mesh axis runs over, the one named last changes fastest.
Arguments:
- wavefield: float32 [4, 4, 16, 32, 9, 512], P('gx', 'gy', 'ha'), may hold values from -6 to 6
- deriv_ops: float32 [3, 512, 512], replicated, may hold values from -0.25 to 0.25
- density: float32 [4, 4, 16, 32], P('gx', 'gy', 'ha'), may hold values from 1 to 3
- lame_first: float32 [4, 4, 16, 32], P('gx', 'gy', 'ha'), may hold values from 0.5 to 2
- shear_modulus: float32 [4, 4, 16, 32], P('gx', 'gy', 'ha'), may hold values from 0.3 to 1
- high_order: int32 [4, 4, 16, 32], P('gx', 'gy', 'ha'), may hold values from 0 to 1, as said below
- element_cell: int32 [4, 4, 16, 32], P('gx', 'gy', 'ha'), may hold values from 0 to 31, each once within a row
- face_orient: int32 [4, 4, 16, 6, 32], P('gx', 'gy', 'ha'), may hold values from 0 to 7
Outputs:
- advanced: float32 [4, 4, 16, 32, 9, 512], P('gx', 'gy', 'ha')
The draws below stay inside these ranges and needn't reach their ends.
Inputs may be any that keep to these rules, and one draw needn't show every extreme that they name: `high_order`: within each group of devices along ha that share gx and gy, exactly half of the devices have 16 flagged elements and the others none; which devices and which elements are drawn. `element_cell`: on every device a permutation of the cells 0 to 31.
All inputs are finite; a program needn't handle non-finite values.
Results may differ from the reference program's by a relative error of at most 0.0001.
Values sent between devices are 32-bit elements; how exact they have to be, the bound alone decides.
A program may use at most 128 MiB of HBM per device.

```python
import math
import jax
import jax.numpy as jnp
from jax import lax

P_SIZE = 8
NODES = 512
FIELDS = 9
EXY = 4
EZ = 2
E_DEV = 32
HOT = 16
STEPS = 2
N_GX = 4
N_GY = 4
N_HA = 16


def shuffled_devices(one_key):
    return jax.random.permutation(one_key, N_HA)


def shuffled_elements(one_key):
    return jax.random.permutation(one_key, E_DEV)


def draw_high_order(key, part):
    base_key = jax.random.fold_in(key, 7)
    heavy_key, element_key = jax.random.split(base_key)
    column_count = N_GX * N_GY
    heavy_keys = jax.random.split(heavy_key, column_count)
    overloaded = jax.vmap(shuffled_devices)(heavy_keys) < N_HA // 2
    element_keys = jax.random.split(element_key, column_count * N_HA)
    element_ranks = jax.vmap(shuffled_elements)(element_keys)
    marked = (element_ranks < HOT) & overloaded.reshape(column_count * N_HA, 1)
    return marked.astype(jnp.int32).reshape(N_GX, N_GY, N_HA, E_DEV)


def place_ends(values, rng, low, largest):
    spot = [jax.random.randint(jax.random.fold_in(rng, axis), (), 0, length) for axis, length in enumerate(values.shape)]
    main_axis = values.shape.index(max(values.shape))
    beside = spot[:main_axis] + [(spot[main_axis] + 1) % values.shape[main_axis]] + spot[main_axis + 1:]
    return values.at[tuple(spot)].set(low).at[tuple(beside)].set(largest)


def steps_of(stream_key, extent, cuts, smallest, top_value):
    loudness, own = 1.0, jax.random.fold_in(stream_key, 6)
    for axis_at, shards_of in cuts:
        heights = jnp.exp(jax.random.uniform(jax.random.fold_in(own, axis_at), (shards_of,), jnp.float32, smallest / len(cuts), top_value / len(cuts)))
        loudness = loudness * jnp.repeat(heights, extent[axis_at] // shards_of).reshape([-1 if axis == axis_at else 1 for axis in range(len(extent))])
    return loudness


def normal_values(own_key, shape, width, most, cuts=(), dtype=jnp.bfloat16):
    entries = jax.random.normal(own_key, shape, jnp.float32) * width
    if len(cuts) > 0:
        entries = steps_of(own_key, shape, cuts, -0.22, 0.18) * entries
    return jnp.clip(entries, min=-most, max=most).astype(dtype)


def setup_inputs(seed: int = 0) -> dict:
    keys = jax.random.split(jax.random.key(seed), 9)
    wavefield = normal_values(keys[0], (N_GX, N_GY, N_HA, E_DEV, FIELDS, NODES), 1.0, 6.0, ((0, 4), (1, 4), (2, 16)), jnp.float32)
    deriv_ops = normal_values(keys[1], (3, NODES, NODES), NODES ** -0.5, 0.25, (), jnp.float32)
    density = jnp.clip(jnp.exp(math.log(3.0) - 1.0986123 * jax.random.uniform(keys[2], (N_GX, N_GY, N_HA, E_DEV), jnp.float32) ** steps_of(keys[2], (N_GX, N_GY, N_HA, E_DEV), ((0, 4), (1, 4), (2, 16)), -0.2, 0.2)), 1.0, 3.0)
    lame_first = jnp.clip(jnp.exp(math.log(2.0) - 1.3862944 * jax.random.uniform(keys[3], (N_GX, N_GY, N_HA, E_DEV), jnp.float32) ** steps_of(keys[3], (N_GX, N_GY, N_HA, E_DEV), ((0, 4), (1, 4), (2, 16)), -0.2, 0.2)), 0.5, 2.0)
    shear_modulus = jnp.clip(jnp.exp(math.log(1.0) - 1.2039728 * jax.random.uniform(keys[4], (N_GX, N_GY, N_HA, E_DEV), jnp.float32) ** steps_of(keys[4], (N_GX, N_GY, N_HA, E_DEV), ((0, 4), (1, 4), (2, 16)), -0.2, 0.2)), 0.3, 1.0)
    high_order = draw_high_order(jax.random.fold_in(keys[8], 71), 0)
    element_cell = jax.vmap(lambda own: jax.random.permutation(own, E_DEV))(jax.random.split(keys[6], N_GX * N_GY * N_HA)).reshape((N_GX, N_GY, N_HA, E_DEV)).astype(jnp.int32)
    face_orient = place_ends(jax.random.randint(keys[7], (N_GX, N_GY, N_HA, 6, E_DEV), 0, 8), jax.random.fold_in(keys[7], 1), 0, 7).astype(jnp.int32)
    return dict(wavefield=wavefield, deriv_ops=deriv_ops, density=density, lame_first=lame_first, shear_modulus=shear_modulus, high_order=high_order, element_cell=element_cell, face_orient=face_orient)


X_FIELDS = (0, 1, 2, 3, 6, 8)
Y_FIELDS = (0, 1, 2, 6, 4, 7)
Z_FIELDS = (0, 1, 2, 8, 7, 5)
DT_STEP = 0.8
LIFT_COEF = 2.0

def derive_along(field_rows, deriv_ops, picked, axis_index):
    chosen = field_rows[..., list(picked), :]
    return jnp.dot(chosen, deriv_ops[axis_index], precision=lax.Precision.HIGHEST, preferred_element_type=jnp.float32)

def time_rate(field_rows, inv_density, lame_coef, shear_coef, deriv_ops):
    x_deriv = derive_along(field_rows, deriv_ops, X_FIELDS, 0)
    y_deriv = derive_along(field_rows, deriv_ops, Y_FIELDS, 1)
    z_deriv = derive_along(field_rows, deriv_ops, Z_FIELDS, 2)
    inv_rho = inv_density[..., None]
    lame_col = lame_coef[..., None]
    shear_col = shear_coef[..., None]
    div_vel = x_deriv[..., 0, :] + y_deriv[..., 1, :] + z_deriv[..., 2, :]
    rate_rows = [inv_rho * (x_deriv[..., 3, :] + y_deriv[..., 3, :] + z_deriv[..., 3, :]), inv_rho * (x_deriv[..., 4, :] + y_deriv[..., 4, :] + z_deriv[..., 4, :]), inv_rho * (x_deriv[..., 5, :] + y_deriv[..., 5, :] + z_deriv[..., 5, :]), lame_col * div_vel + 2.0 * shear_col * x_deriv[..., 0, :], lame_col * div_vel + 2.0 * shear_col * y_deriv[..., 1, :], lame_col * div_vel + 2.0 * shear_col * z_deriv[..., 2, :], shear_col * (x_deriv[..., 1, :] + y_deriv[..., 0, :]), shear_col * (y_deriv[..., 2, :] + z_deriv[..., 1, :]), shear_col * (x_deriv[..., 2, :] + z_deriv[..., 0, :])]
    return jnp.stack(rate_rows, axis=-2)

def normal_flux(jump_face, inv_rho, lame_col, shear_col, direction):
    parts_list = [jump_face[..., index_value, :] for index_value in range(9)]
    zeros_face = jnp.zeros_like(parts_list[0])
    stiff_col = lame_col + 2.0 * shear_col
    if direction == 0:
        rows_out = [inv_rho * parts_list[3], inv_rho * parts_list[6], inv_rho * parts_list[8], stiff_col * parts_list[0], lame_col * parts_list[0], lame_col * parts_list[0], shear_col * parts_list[1], zeros_face, shear_col * parts_list[2]]
    elif direction == 1:
        rows_out = [inv_rho * parts_list[6], inv_rho * parts_list[4], inv_rho * parts_list[7], lame_col * parts_list[1], stiff_col * parts_list[1], lame_col * parts_list[1], shear_col * parts_list[0], shear_col * parts_list[2], zeros_face]
    else:
        rows_out = [inv_rho * parts_list[8], inv_rho * parts_list[7], inv_rho * parts_list[5], lame_col * parts_list[2], lame_col * parts_list[2], stiff_col * parts_list[2], zeros_face, shear_col * parts_list[1], shear_col * parts_list[0]]
    return -jnp.stack(rows_out, axis=-2)

def face_select(edge_nodes):
    node_count = edge_nodes ** 3
    face_nodes = edge_nodes * edge_nodes
    node_ids = jnp.arange(node_count)
    first_index = node_ids // face_nodes
    second_index = node_ids // edge_nodes % edge_nodes
    third_index = node_ids % edge_nodes
    column_ids = jnp.arange(6 * face_nodes)
    layout = [(first_index == 0, second_index, third_index), (first_index == edge_nodes - 1, second_index, third_index), (second_index == 0, first_index, third_index), (second_index == edge_nodes - 1, first_index, third_index), (third_index == 0, first_index, second_index), (third_index == edge_nodes - 1, first_index, second_index)]
    face_table = jnp.zeros((node_count, 6 * face_nodes), jnp.float32)
    for face_index in range(6):
        on_face, row_pos, col_pos = layout[face_index]
        target = face_index * face_nodes + row_pos * edge_nodes + col_pos
        picked = (column_ids[None, :] == target[:, None]) & on_face[:, None]
        face_table = face_table + picked.astype(jnp.float32)
    return face_table

def orient_faces(outside, orient_codes, edge_nodes):
    face_grid = outside.reshape(outside.shape[:-1] + (edge_nodes, edge_nodes))
    result = jnp.zeros_like(face_grid)
    for orient_code in range(8):
        variant = face_grid
        if orient_code & 4:
            variant = jnp.swapaxes(variant, -1, -2)
        if orient_code & 1:
            variant = jnp.flip(variant, -2)
        if orient_code & 2:
            variant = jnp.flip(variant, -1)
        result = jnp.where((orient_codes == orient_code)[..., None, None], variant, result)
    return result.reshape(outside.shape)

def face_correction(own_traces, oriented, inv_density, lame_coef, shear_coef):
    inv_rho = inv_density[..., None]
    lame_col = lame_coef[..., None]
    shear_col = shear_coef[..., None]
    wave_speed = jnp.sqrt((lame_col + 2.0 * shear_col) * inv_rho)
    trace_jump = oriented - own_traces
    corrections = []
    for face_index in range(6):
        normal_sign = -1.0 if face_index % 2 == 0 else 1.0
        jump_face = trace_jump[..., face_index, :]
        flux_face = normal_flux(jump_face, inv_rho, lame_col, shear_col, face_index // 2)
        corrections.append(0.5 * (wave_speed[..., None] * jump_face - normal_sign * flux_face))
    return jnp.stack(corrections, axis=-2)

def extra_series(start_rows, inv_density, lame_coef, shear_coef, deriv_ops):
    series_term = start_rows
    series_sum = jnp.zeros_like(start_rows)
    for order_index in (3, 4, 5):
        series_term = time_rate(series_term, inv_density, lame_coef, shear_coef, deriv_ops)
        series_sum = series_sum + DT_STEP ** order_index / math.factorial(order_index + 1) * series_term
    return series_sum

def shift_along(block, axis_index, from_lower):
    zero_layer = jnp.zeros_like(lax.slice_in_dim(block, 0, 1, axis=axis_index))
    length = block.shape[axis_index]
    if from_lower:
        return jnp.concatenate([zero_layer, lax.slice_in_dim(block, 0, length - 1, axis=axis_index)], axis=axis_index)
    return jnp.concatenate([lax.slice_in_dim(block, 1, length, axis=axis_index), zero_layer], axis=axis_index)

def reference(wavefield, deriv_ops, density, lame_first, shear_modulus, high_order, element_cell, face_orient):
    face_table = face_select(P_SIZE)
    face_nodes = P_SIZE * P_SIZE
    inv_density = 1.0 / density
    orient_codes = jnp.swapaxes(face_orient, -1, -2)[..., None, :]
    row_total = N_GX * N_GY * N_HA * E_DEV
    flat_flagged = jnp.nonzero(high_order.reshape(-1), size=N_GX * N_GY * N_HA // 2 * HOT)[0].astype(jnp.int32)
    inverse = jnp.argsort(element_cell, axis=-1).astype(jnp.int32)
    cell_index = element_cell.astype(jnp.int32)
    flat_inv = inv_density.reshape(row_total)[flat_flagged]
    flat_lame = lame_first.reshape(row_total)[flat_flagged]
    flat_shear = shear_modulus.reshape(row_total)[flat_flagged]
    current = wavefield
    for step_index in range(STEPS):
        first_rate = time_rate(current, inv_density, lame_first, shear_modulus, deriv_ops)
        second_rate = time_rate(first_rate, inv_density, lame_first, shear_modulus, deriv_ops)
        integrated = current + DT_STEP / 2.0 * first_rate + DT_STEP ** 2 / 6.0 * second_rate
        flat_second = second_rate.reshape(row_total, FIELDS, NODES)[flat_flagged]
        extra_term = extra_series(flat_second, flat_inv, flat_lame, flat_shear, deriv_ops)
        integrated = integrated.reshape(row_total, FIELDS, NODES).at[flat_flagged].add(extra_term).reshape(current.shape)
        traces = jnp.dot(integrated, face_table, precision=lax.Precision.HIGHEST, preferred_element_type=jnp.float32)
        cell_traces = jnp.take_along_axis(traces, inverse[..., None, None], axis=3)
        cell_brick = cell_traces.reshape(N_GX, N_GY, N_HA, EXY, EXY, EZ, FIELDS, 6, face_nodes)
        cell_brick = cell_brick.transpose(0, 3, 1, 4, 2, 5, 6, 7, 8).reshape(N_GX * EXY, N_GY * EXY, N_HA * EZ, FIELDS, 6, face_nodes)
        outside_list = [shift_along(cell_brick[..., 1, :], 0, True), shift_along(cell_brick[..., 0, :], 0, False), shift_along(cell_brick[..., 3, :], 1, True), shift_along(cell_brick[..., 2, :], 1, False), shift_along(cell_brick[..., 5, :], 2, True), shift_along(cell_brick[..., 4, :], 2, False)]
        outside = jnp.stack(outside_list, axis=-2)
        outside = outside.reshape(N_GX, EXY, N_GY, EXY, N_HA, EZ, FIELDS, 6, face_nodes)
        outside = outside.transpose(0, 2, 4, 1, 3, 5, 6, 7, 8).reshape(N_GX, N_GY, N_HA, E_DEV, FIELDS, 6, face_nodes)
        outside = jnp.take_along_axis(outside, cell_index[..., None, None, None], axis=3)
        oriented = orient_faces(outside, orient_codes, P_SIZE)
        own_traces = traces.reshape(N_GX, N_GY, N_HA, E_DEV, FIELDS, 6, face_nodes)
        correction = face_correction(own_traces, oriented, inv_density, lame_first, shear_modulus)
        correction = correction.reshape(N_GX, N_GY, N_HA, E_DEV, FIELDS, 6 * face_nodes)
        lifted = jnp.dot(correction, face_table.T, precision=lax.Precision.HIGHEST, preferred_element_type=jnp.float32)
        volume_rate = time_rate(integrated, inv_density, lame_first, shear_modulus, deriv_ops)
        current = current + DT_STEP * (volume_rate + LIFT_COEF * lifted)
    return current
```

```python
import math

import jax
import jax.numpy as jnp
from jax import lax
from jax.experimental import pallas as pl
from jax.experimental.pallas import tpu as pltpu
from jax.sharding import PartitionSpec as P

ELEMENTS = 32
FIELDS = 9
NODES = 512
STEPS = 2
DT_STEP = 0.8
LIFT_COEF = 2.0
X_FIELDS = (0, 1, 2, 3, 6, 8)
Y_FIELDS = (0, 1, 2, 6, 4, 7)
Z_FIELDS = (0, 1, 2, 8, 7, 5)
AXIS_FIELDS = (X_FIELDS, Y_FIELDS, Z_FIELDS)
MESH_AXES = ("gx", "gy", "ha")
SERIES = tuple(DT_STEP**k / math.factorial(k + 1) for k in range(6))
F32 = jnp.float32
BF16 = jnp.bfloat16
I32 = jnp.int32
NT = (((1,), (1,)), ((), ()))
HIGHEST = lax.Precision.HIGHEST


def dot(a, b):
    return jnp.dot(a, b, preferred_element_type=F32)


def halves(value):
    high = value.astype(BF16)
    return high, (value - high.astype(F32)).astype(BF16)


def thirds(value):
    high = value.astype(BF16)
    rest = value - high.astype(F32)
    mid = rest.astype(BF16)
    return high, mid, (rest - mid.astype(F32)).astype(BF16)


def rows_of(field):
    return slice(ELEMENTS * field, ELEMENTS * (field + 1))


def iota(shape, dim):
    return lax.broadcasted_iota(I32, shape, dim)


def face_node(column):
    face = column // 64
    p = (column // 8) % 8
    r = column % 8
    far = 7 * (face % 2)
    return jnp.where(face < 2, p * 64 + far * 8 + r, p * 64 + r * 8 + far)


def kernel(
    wave, dops, dens, lame, shear, hot, cell, orient, out,
    wf, wh, wl, small, coef, flags, index, q, acc, xh, xl, deriv, pick, lift, tr, ch, cl, cx,
    send_x, send_y, send_z, recv_x, recv_y, recv_z, load_sem, send_sem, recv_sem,
):
    barrier = pltpu.get_barrier_semaphore()
    place = [lax.axis_index(a) for a in MESH_AXES]
    count = [lax.axis_size(a) for a in MESH_AXES]
    up = [{a: lax.rem(i + 1, n)} for a, i, n in zip(MESH_AXES, place, count)]
    down = [{a: lax.rem(i + n - 1, n)} for a, i, n in zip(MESH_AXES, place, count)]
    for target in up + down:
        pl.semaphore_signal(barrier, 1, device_id=target, device_id_type=pl.DeviceIdType.MESH)

    loads = [pltpu.make_async_copy(dops.at[a], wf.at[a], load_sem.at[a]) for a in range(3)]
    for load in loads:
        load.start()

    small[...] = jnp.zeros_like(small)
    small[0:1, :] = dens[...]
    small[1:2, :] = lame[...]
    small[2:3, :] = shear[...]
    small[3:4, :] = hot[...].astype(F32)
    small[4:10, :] = orient[...].astype(F32)
    small[10:11, :] = cell[...].astype(F32)
    square = (ELEMENTS, ELEMENTS)
    place_cell = (iota(square, 0) == jnp.broadcast_to(cell[...], square)).astype(F32)
    by_cell = lax.dot_general(place_cell, small[...], NT, precision=HIGHEST)
    same = (iota(square, 0) == iota(square, 1)).astype(F32)
    by_element = lax.dot_general(same, small[...], NT, precision=HIGHEST)
    wide = (ELEMENTS, 128)
    inv_rho = 1.0 / by_cell[:, 0:1]
    lame_col = by_cell[:, 1:2]
    shear_col = by_cell[:, 2:3]
    coef[0] = jnp.broadcast_to(inv_rho, wide)
    coef[1] = jnp.broadcast_to(lame_col, wide)
    coef[2] = jnp.broadcast_to(shear_col, wide)
    coef[3] = jnp.broadcast_to(jnp.sqrt((lame_col + 2.0 * shear_col) * inv_rho), wide)
    flags[...] = jnp.broadcast_to(by_cell[:, 3:4], wide)
    lane = iota(wide, 1)
    p_pos = (lane // 8) % 8
    r_pos = lane % 8
    for d in range(3):
        low = jnp.broadcast_to(by_cell[:, 4 + 2 * d : 5 + 2 * d], wide)
        high = jnp.broadcast_to(by_cell[:, 5 + 2 * d : 6 + 2 * d], wide)
        code = jnp.where(lane < 64, low, high).astype(I32)
        p_src = jnp.where((code & 1) != 0, 7 - p_pos, p_pos)
        r_src = jnp.where((code & 2) != 0, 7 - r_pos, r_pos)
        node = jnp.where((code & 4) != 0, r_src * 8 + p_src, p_src * 8 + r_src)
        index[d] = node + jnp.where(lane < 64, 64, 0)
    pick[...] = (iota((NODES, 256), 0) == face_node(iota((NODES, 256), 1))).astype(BF16)
    lift[...] = (iota((256, NODES), 1) == face_node(iota((256, NODES), 0))).astype(BF16)
    gather_in = place_cell.astype(BF16)
    for f in range(FIELDS):
        a, b, c = thirds(wave[f])
        q[f] = dot(gather_in, a) + dot(gather_in, b) + dot(gather_in, c)

    for a in range(3):
        loads[a].wait()

        def split(i, carry, a=a):
            part = pl.ds(pl.multiple_of(i * 64, 64), 64)
            h, l = halves(wf[a, part, :])
            wh[a, part, :] = h
            wl[a, part, :] = l
            return carry

        lax.fori_loop(0, NODES // 64, split, 0)

    for recv, at, n in zip((recv_x, recv_y, recv_z), place, count):
        for edge, slot in ((0, 0), (n - 1, 1)):

            @pl.when(at == edge)
            def _(recv=recv, slot=slot):
                for s in range(STEPS):
                    recv[s, slot] = jnp.zeros_like(recv[s, slot])

    def set_operand(source):
        for f in range(FIELDS):
            xh[rows_of(f), :], xl[rows_of(f), :] = halves(source[f])

    def derive():
        for a, fields in enumerate(AXIS_FIELDS):
            h = jnp.concatenate([xh[rows_of(f), :] for f in fields], axis=0)
            l = jnp.concatenate([xl[rows_of(f), :] for f in fields], axis=0)
            deriv[a] = dot(h, wh[a]) + dot(l, wh[a]) + dot(h, wl[a])

    def rates(part):
        x = [deriv[0, rows_of(i), part] for i in range(6)]
        y = [deriv[1, rows_of(i), part] for i in range(6)]
        z = [deriv[2, rows_of(i), part] for i in range(6)]
        inv, lam, mu = coef[0], coef[1], coef[2]
        lam_div = lam * (x[0] + y[1] + z[2])
        mu2 = 2.0 * mu
        return [
            inv * (x[3] + y[3] + z[3]),
            inv * (x[4] + y[4] + z[4]),
            inv * (x[5] + y[5] + z[5]),
            lam_div + mu2 * x[0],
            lam_div + mu2 * y[1],
            lam_div + mu2 * z[2],
            mu * (x[1] + y[0]),
            mu * (y[2] + z[1]),
            mu * (x[2] + z[0]),
        ]

    def advance(first, weight, only_flagged):
        derive()
        for j in range(4):
            part = slice(128 * j, 128 * (j + 1))
            for f, rate in enumerate(rates(part)):
                term = weight * rate
                if only_flagged:
                    term = jnp.where(flags[...] > 0.5, term, 0.0)
                base = q if first else acc
                acc[f, :, part] = base[f, :, part] + term
                xh[rows_of(f), part], xl[rows_of(f), part] = halves(rate)

    def pack_pairs(tile, upper, dest):
        keep = (iota((8, 128), 1) >= 64) if upper else (iota((8, 128), 1) < 64)
        for f in range(4):
            dest[f] = jnp.where(keep, tile(f), pltpu.roll(tile(f + 5), 64, 1))
        dest[4] = tile(4)

    def unpack_pairs(source, f):
        return source[f] if f < 5 else pltpu.roll(source[f - 5], 64, 1)

    sub = iota((8, 128), 0)
    lo_lane = iota((8, 128), 1) < 64
    even = sub % 2 == 0

    def pack_rows_y(f, first_row):
        result = None
        for a in range(4):
            tile = tr[1, f, 8 * a : 8 * a + 8, :]
            shift = (2 * a - first_row) % 8
            moved = pltpu.roll(tile, shift, 0) if shift else tile
            result = moved if a == 0 else jnp.where(sub // 2 == a, moved, result)
        return result

    def pack_z(f, odd):
        strips = []
        for a in range(2):
            one = tr[2, f, 8 * a : 8 * a + 8, :]
            two = tr[2, f, 8 * a + 16 : 8 * a + 24, :]
            if odd:
                strips.append(jnp.where(even, pltpu.roll(two, 7, 0), one))
            else:
                strips.append(jnp.where(even, one, pltpu.roll(two, 1, 0)))
        keep = jnp.logical_not(lo_lane) if odd else lo_lane
        return jnp.where(keep, strips[0], pltpu.roll(strips[1], 64, 1))

    sends = (send_x, send_y, send_z)
    recvs = (recv_x, recv_y, recv_z)

    def copies(step):
        made = []
        for d in range(3):
            for way, target in ((0, up[d]), (1, down[d])):
                made.append(
                    pltpu.make_async_remote_copy(
                        src_ref=sends[d].at[way],
                        dst_ref=recvs[d].at[step, way],
                        send_sem=send_sem.at[step, 2 * d + way],
                        recv_sem=recv_sem.at[step, 2 * d + way],
                        device_id=target,
                        device_id_type=pl.DeviceIdType.MESH,
                    )
                )
        return made

    def sending(k):
        d, way = divmod(k, 2)
        return place[d] < count[d] - 1 if way == 0 else place[d] > 0

    def receiving(k):
        d, way = divmod(k, 2)
        return place[d] > 0 if way == 0 else place[d] < count[d] - 1

    def neighbours(step, d, f, a):
        tile = tr[d, f, 8 * a : 8 * a + 8, :]
        if d == 0:
            before = unpack_pairs(recv_x.at[step, 0], f) if a == 0 else tr[0, f, 8 * a - 8 : 8 * a, :]
            after = unpack_pairs(recv_x.at[step, 1], f) if a == 3 else tr[0, f, 8 * a + 8 : 8 * a + 16, :]
        elif d == 1:
            low = unpack_pairs(recv_y.at[step, 0], f)
            low = pltpu.roll(low, (8 - 2 * a) % 8, 0) if a else low
            before = jnp.where(sub < 2, low, pltpu.roll(tile, 2, 0))
            high = unpack_pairs(recv_y.at[step, 1], f)
            high = pltpu.roll(high, (6 - 2 * a) % 8, 0) if a < 3 else high
            after = jnp.where(sub >= 6, high, pltpu.roll(tile, 6, 0))
        else:
            low = recv_z[step, 0, f]
            high = recv_z[step, 1, f]
            if a % 2:
                low = pltpu.roll(low, 64, 1)
                high = pltpu.roll(high, 64, 1)
            if a < 2:
                low = pltpu.roll(low, 7, 0)
                high = pltpu.roll(high, 1, 0)
            before = jnp.where(even, low, pltpu.roll(tile, 1, 0))
            after = jnp.where(even, pltpu.roll(tile, 7, 0), high)
        return jnp.where(lo_lane, after, before)

    def corrections(step):
        sign = jnp.where(lo_lane, -1.0, 1.0)
        for d in range(3):
            for a in range(4):
                rows = slice(8 * a, 8 * a + 8)
                source = index[d, rows, :]
                w = [
                    jnp.take_along_axis(neighbours(step, d, f, a), source, axis=1) - tr[d, f, rows, :]
                    for f in range(FIELDS)
                ]
                inv, lam, mu, speed = [coef[i, rows, :] for i in range(4)]
                stiff = lam + 2.0 * mu
                if d == 0:
                    lam_v = lam * w[0]
                    flux = [inv * w[3], inv * w[6], inv * w[8], stiff * w[0], lam_v, lam_v,
                            mu * w[1], None, mu * w[2]]
                elif d == 1:
                    lam_v = lam * w[1]
                    flux = [inv * w[6], inv * w[4], inv * w[7], lam_v, stiff * w[1], lam_v,
                            mu * w[0], mu * w[2], None]
                else:
                    lam_v = lam * w[2]
                    flux = [inv * w[8], inv * w[7], inv * w[5], lam_v, lam_v, stiff * w[2],
                            None, mu * w[1], mu * w[0]]
                for f in range(FIELDS):
                    fixed = speed * w[f]
                    if flux[f] is not None:
                        fixed = fixed + sign * flux[f]
                    fixed = 0.5 * fixed
                    if d == 0:
                        cx[f, rows, :] = fixed
                    else:
                        tr[d, f, rows, :] = fixed
        for d in (1, 2):
            part = slice(128 * (d - 1), 128 * d)
            for f in range(FIELDS):
                ch[rows_of(f), part], cl[rows_of(f), part] = halves(tr[d, f])

    def step_body(step, carry):
        set_operand(q)
        advance(True, SERIES[1], False)
        advance(False, SERIES[2], False)

        def higher(k, c):
            weight = jnp.where(k == 0, SERIES[3], jnp.where(k == 1, SERIES[4], SERIES[5]))
            advance(False, weight.astype(F32), True)
            return c

        lax.fori_loop(0, 3, higher, 0)
        set_operand(acc)
        faces = dot(xh[...], pick[...]) + dot(xl[...], pick[...])
        for f in range(FIELDS):
            lower = acc[f, :, 0:128]
            upper = acc[f, :, 384:512]
            tr[0, f] = jnp.where(lane < 64, lower, upper)
            tr[1, f] = faces[rows_of(f), 0:128]
            tr[2, f] = faces[rows_of(f), 128:256]
        pack_pairs(lambda f: tr[0, f, 24:32, :], True, send_x.at[0])
        pack_pairs(lambda f: tr[0, f, 0:8, :], False, send_x.at[1])
        pack_pairs(lambda f: pack_rows_y(f, 6), True, send_y.at[0])
        pack_pairs(lambda f: pack_rows_y(f, 0), False, send_y.at[1])
        for f in range(FIELDS):
            send_z[0, f] = pack_z(f, True)
            send_z[1, f] = pack_z(f, False)

        @pl.when(step == 0)
        def _():
            pl.semaphore_wait(barrier, 6)

        made = copies(step)
        for k in range(6):

            @pl.when(sending(k))
            def _(k=k):
                made[k].start()

        derive()
        for k in range(6):

            @pl.when(receiving(k))
            def _(k=k):
                made[k].wait_recv()

        corrections(step)
        for j in range(4):
            part = slice(128 * j, 128 * (j + 1))
            for f, rate in enumerate(rates(part)):
                lifted = dot(ch[rows_of(f), :], lift[:, part]) + dot(cl[rows_of(f), :], lift[:, part])
                if j == 0:
                    lifted = lifted + jnp.where(lane < 64, cx[f], 0.0)
                if j == 3:
                    lifted = lifted + jnp.where(lane < 64, 0.0, cx[f])
                q[f, :, part] = q[f, :, part] + DT_STEP * (rate + LIFT_COEF * lifted)
        for k in range(6):

            @pl.when(sending(k))
            def _(k=k):
                made[k].wait_send()

        return carry

    lax.fori_loop(0, STEPS, step_body, 0)
    gather_out = (by_element[:, 10:11].astype(I32) == iota(square, 1)).astype(BF16)
    for f in range(FIELDS):
        a, b, c = thirds(q[f])
        out[f] = dot(gather_out, a) + dot(gather_out, b) + dot(gather_out, c)


def shards(
    wavefield, deriv_ops, density, lame_first, shear_modulus, high_order, element_cell, face_orient
):
    wave = jnp.swapaxes(wavefield[0, 0, 0], 0, 1)
    row = (1, ELEMENTS)
    vmem = pl.BlockSpec(memory_space=pltpu.VMEM)
    field = (FIELDS, ELEMENTS, NODES)
    total = FIELDS * ELEMENTS
    result = pl.pallas_call(
        kernel,
        out_shape=jax.ShapeDtypeStruct(field, F32),
        in_specs=[vmem, pl.BlockSpec(memory_space=pl.ANY)] + [vmem] * 6,
        out_specs=vmem,
        scratch_shapes=[
            pltpu.VMEM((3, NODES, NODES), F32),
            pltpu.VMEM((3, NODES, NODES), BF16),
            pltpu.VMEM((3, NODES, NODES), BF16),
            pltpu.VMEM((16, ELEMENTS), F32),
            pltpu.VMEM((4, ELEMENTS, 128), F32),
            pltpu.VMEM((ELEMENTS, 128), F32),
            pltpu.VMEM((3, ELEMENTS, 128), I32),
            pltpu.VMEM(field, F32),
            pltpu.VMEM(field, F32),
            pltpu.VMEM((total, NODES), BF16),
            pltpu.VMEM((total, NODES), BF16),
            pltpu.VMEM((3, 6 * ELEMENTS, NODES), F32),
            pltpu.VMEM((NODES, 256), BF16),
            pltpu.VMEM((256, NODES), BF16),
            pltpu.VMEM((3, FIELDS, ELEMENTS, 128), F32),
            pltpu.VMEM((total, 256), BF16),
            pltpu.VMEM((total, 256), BF16),
            pltpu.VMEM((FIELDS, ELEMENTS, 128), F32),
            pltpu.VMEM((2, 5, 8, 128), F32),
            pltpu.VMEM((2, 5, 8, 128), F32),
            pltpu.VMEM((2, FIELDS, 8, 128), F32),
            pltpu.VMEM((STEPS, 2, 5, 8, 128), F32),
            pltpu.VMEM((STEPS, 2, 5, 8, 128), F32),
            pltpu.VMEM((STEPS, 2, FIELDS, 8, 128), F32),
            pltpu.SemaphoreType.DMA((3,)),
            pltpu.SemaphoreType.DMA((STEPS, 6)),
            pltpu.SemaphoreType.DMA((STEPS, 6)),
        ],
        compiler_params=pltpu.CompilerParams(
            collective_id=0, has_side_effects=True, vmem_limit_bytes=60 * 1024 * 1024
        ),
        name="elastic_steps",
    )(
        wave,
        deriv_ops,
        density.reshape(row),
        lame_first.reshape(row),
        shear_modulus.reshape(row),
        high_order.reshape(row),
        element_cell.reshape(row),
        face_orient.reshape(6, ELEMENTS),
    )
    return jnp.swapaxes(result, 0, 1)[None, None, None]


def solution(mesh):
    row = P("gx", "gy", "ha", None)
    whole = P("gx", "gy", "ha", None, None, None)
    return jax.shard_map(
        shards,
        mesh=mesh,
        in_specs=(whole, P(), row, row, row, row, row, P("gx", "gy", "ha", None, None)),
        out_specs=whole,
        check_vma=False,
    )
```

```python
import math

import jax
import jax.numpy as jnp
from jax import lax
from jax.experimental import pallas as pl
from jax.experimental.pallas import tpu as pltpu
from jax.sharding import PartitionSpec as P

ELEMENTS = 32
HOT = 16
FIELDS = 9
NODES = 512
STEPS = 2
DT_STEP = 0.8
LIFT_COEF = 2.0
X_FIELDS = (0, 1, 2, 3, 6, 8)
Y_FIELDS = (0, 1, 2, 6, 4, 7)
Z_FIELDS = (0, 1, 2, 8, 7, 5)
AXIS_FIELDS = (X_FIELDS, Y_FIELDS, Z_FIELDS)
MESH_AXES = ("gx", "gy", "ha")
SERIES = tuple(DT_STEP**k / math.factorial(k + 1) for k in range(6))
F32 = jnp.float32
BF16 = jnp.bfloat16
I32 = jnp.int32
NT = (((1,), (1,)), ((), ()))
HIGHEST = lax.Precision.HIGHEST


def dot(a, b):
    return jnp.dot(a, b, preferred_element_type=F32)


def halves(value):
    high = value.astype(BF16)
    return high, (value - high.astype(F32)).astype(BF16)


def thirds(value):
    high = value.astype(BF16)
    rest = value - high.astype(F32)
    mid = rest.astype(BF16)
    return high, mid, (rest - mid.astype(F32)).astype(BF16)


def rows_of(field):
    return slice(ELEMENTS * field, ELEMENTS * (field + 1))


def iota(shape, dim):
    return lax.broadcasted_iota(I32, shape, dim)


def face_node(column):
    face = column // 64
    p = (column // 8) % 8
    r = column % 8
    far = 7 * (face % 2)
    return jnp.where(face < 2, p * 64 + far * 8 + r, p * 64 + r * 8 + far)


def kernel(
    wave_in, dops, dens_in, lame_in, shear_in, hot_in, cell_in, orient_in, out,
    wave, dens, lame, shear, hot, cell, orient,
    wf, wh, wl, small, coef, index, q, acc, xh, xl, deriv, pick, lift, tr, ch, cl, cx,
    hot_in_rows, hot_coef, hot_sum, yh, yl, hot_deriv, hot_sel,
    send_x, send_y, send_z, recv_x, recv_y, recv_z, small_sem, load_sem, send_sem, recv_sem,
):
    barrier = pltpu.get_barrier_semaphore()
    place = [lax.axis_index(a) for a in MESH_AXES]
    count = [lax.axis_size(a) for a in MESH_AXES]
    up = [{a: lax.rem(i + 1, n)} for a, i, n in zip(MESH_AXES, place, count)]
    down = [{a: lax.rem(i + n - 1, n)} for a, i, n in zip(MESH_AXES, place, count)]
    for target in up + down:
        pl.semaphore_signal(barrier, 1, device_id=target, device_id_type=pl.DeviceIdType.MESH)

    small_loads = [
        pltpu.make_async_copy(source, dest, small_sem.at[i])
        for i, (source, dest) in enumerate(
            (
                (cell_in, cell), (hot_in, hot), (dens_in, dens), (lame_in, lame),
                (shear_in, shear), (orient_in, orient), (wave_in, wave),
            )
        )
    ]
    for load in small_loads:
        load.start()
    loads = [pltpu.make_async_copy(dops.at[a], wf.at[a], load_sem.at[a]) for a in range(3)]
    for load in loads:
        load.start()

    small[...] = jnp.zeros_like(small)
    for load in small_loads[:-1]:
        load.wait()
    small[0:1, :] = dens[...]
    small[1:2, :] = lame[...]
    small[2:3, :] = shear[...]
    small[3:4, :] = hot[...].astype(F32)
    for i in range(6):
        small[4 + i : 5 + i, :] = orient[i].astype(F32)
    small[10:11, :] = cell[...].astype(F32)
    square = (ELEMENTS, ELEMENTS)
    place_cell = (iota(square, 0) == jnp.broadcast_to(cell[...], square)).astype(F32)
    by_cell = lax.dot_general(place_cell, small[...], NT, precision=HIGHEST)
    same = (iota(square, 0) == iota(square, 1)).astype(F32)
    by_element = lax.dot_general(same, small[...], NT, precision=HIGHEST)
    wide = (ELEMENTS, 128)
    inv_rho = 1.0 / by_cell[:, 0:1]
    lame_col = by_cell[:, 1:2]
    shear_col = by_cell[:, 2:3]
    coef[0] = jnp.broadcast_to(inv_rho, wide)
    coef[1] = jnp.broadcast_to(lame_col, wide)
    coef[2] = jnp.broadcast_to(shear_col, wide)
    coef[3] = jnp.broadcast_to(jnp.sqrt((lame_col + 2.0 * shear_col) * inv_rho), wide)
    lane = iota(wide, 1)
    p_pos = (lane // 8) % 8
    r_pos = lane % 8
    for d in range(3):
        low = jnp.broadcast_to(by_cell[:, 4 + 2 * d : 5 + 2 * d], wide)
        high = jnp.broadcast_to(by_cell[:, 5 + 2 * d : 6 + 2 * d], wide)
        code = jnp.where(lane < 64, low, high).astype(I32)
        p_src = jnp.where((code & 1) != 0, 7 - p_pos, p_pos)
        r_src = jnp.where((code & 2) != 0, 7 - r_pos, r_pos)
        node = jnp.where((code & 4) != 0, r_src * 8 + p_src, p_src * 8 + r_src)
        index[d] = node + jnp.where(lane < 64, 64, 0)
    pick[...] = (iota((NODES, 256), 0) == face_node(iota((NODES, 256), 1))).astype(BF16)
    lift[...] = (iota((256, NODES), 1) == face_node(iota((256, NODES), 0))).astype(BF16)
    slots = (HOT, ELEMENTS)
    flag_row = lax.dot_general(small[...], place_cell, NT, precision=HIGHEST)[3:4, :]
    upto = (iota(square, 0) <= iota(square, 1)).astype(F32)
    rank_row = lax.dot_general(
        jnp.broadcast_to(flag_row, (8, ELEMENTS)), upto, (((1,), (0,)), ((), ())), precision=HIGHEST
    )[0:1, :].astype(I32)
    chosen = (iota(slots, 0) + 1 == jnp.broadcast_to(rank_row, slots)) & (
        jnp.broadcast_to(flag_row, slots) > 0.5
    )
    select = chosen.astype(F32)
    hot_sel[...] = select.astype(BF16)
    of_slot = lax.dot_general(select, by_cell, (((1,), (0,)), ((), ())), precision=HIGHEST)
    filled = of_slot[:, 0:1] > 0.0
    hot_coef[0] = jnp.broadcast_to(
        jnp.where(filled, 1.0 / jnp.where(filled, of_slot[:, 0:1], 1.0), 0.0), (HOT, 128)
    )
    hot_coef[1] = jnp.broadcast_to(of_slot[:, 1:2], (HOT, 128))
    hot_coef[2] = jnp.broadcast_to(of_slot[:, 2:3], (HOT, 128))
    slot_col = iota((ELEMENTS, HOT), 1) + 1
    below = (iota(square, 1) <= iota(square, 0)).astype(F32)
    rank_col = lax.dot_general(
        below, jnp.broadcast_to(by_cell[:, 3:4], (ELEMENTS, 8)), (((1,), (0,)), ((), ())), precision=HIGHEST
    )[:, 0:1]
    back = (slot_col == rank_col.astype(I32)) & (by_cell[:, 3:4] > 0.5)
    hot_in_rows[...] = back.astype(BF16)
    gather_in = place_cell.astype(BF16)
    small_loads[-1].wait()
    for f in range(FIELDS):
        a, b, c = thirds(wave[f])
        q[f] = dot(gather_in, a) + dot(gather_in, b) + dot(gather_in, c)

    for a in range(3):
        loads[a].wait()

        def split(i, carry, a=a):
            part = pl.ds(pl.multiple_of(i * 64, 64), 64)
            h, l = halves(wf[a, part, :])
            wh[a, part, :] = h
            wl[a, part, :] = l
            return carry

        lax.fori_loop(0, NODES // 64, split, 0)

    for recv, at, n in zip((recv_x, recv_y, recv_z), place, count):
        for edge, slot in ((0, 0), (n - 1, 1)):

            @pl.when(at == edge)
            def _(recv=recv, slot=slot):
                for s in range(STEPS):
                    recv[s, slot] = jnp.zeros_like(recv[s, slot])

    def set_operand(source):
        for f in range(FIELDS):
            xh[rows_of(f), :], xl[rows_of(f), :] = halves(source[f])

    def derive():
        for a, fields in enumerate(AXIS_FIELDS):
            h = jnp.concatenate([xh[rows_of(f), :] for f in fields], axis=0)
            l = jnp.concatenate([xl[rows_of(f), :] for f in fields], axis=0)
            deriv[a] = dot(h, wh[a]) + dot(l, wh[a]) + dot(h, wl[a])

    def hot_rows(field):
        return slice(HOT * field, HOT * (field + 1))

    def derive_hot():
        for a, fields in enumerate(AXIS_FIELDS):
            h = [yh[hot_rows(f), :] for f in fields]
            l = [yl[hot_rows(f), :] for f in fields]
            both = dot(jnp.concatenate(h + l, axis=0), wh[a])
            cross = dot(jnp.concatenate(h, axis=0), wl[a])
            hot_deriv[a] = both[0 : 6 * HOT] + (both[6 * HOT :] + cross)

    def rates(part, source=deriv, rows=rows_of, factors=coef):
        x = [source[0, rows(i), part] for i in range(6)]
        y = [source[1, rows(i), part] for i in range(6)]
        z = [source[2, rows(i), part] for i in range(6)]
        inv, lam, mu = factors[0], factors[1], factors[2]
        lam_div = lam * (x[0] + y[1] + z[2])
        mu2 = 2.0 * mu
        return [
            inv * (x[3] + y[3] + z[3]),
            inv * (x[4] + y[4] + z[4]),
            inv * (x[5] + y[5] + z[5]),
            lam_div + mu2 * x[0],
            lam_div + mu2 * y[1],
            lam_div + mu2 * z[2],
            mu * (x[1] + y[0]),
            mu * (y[2] + z[1]),
            mu * (x[2] + z[0]),
        ]

    def advance(first, weight):
        derive()
        for j in range(4):
            part = slice(128 * j, 128 * (j + 1))
            for f, rate in enumerate(rates(part)):
                term = weight * rate
                base = q if first else acc
                acc[f, :, part] = base[f, :, part] + term
                xh[rows_of(f), part], xl[rows_of(f), part] = halves(rate)

    def pack_pairs(tile, upper, dest):
        keep = (iota((8, 128), 1) >= 64) if upper else (iota((8, 128), 1) < 64)
        for f in range(4):
            dest[f] = jnp.where(keep, tile(f), pltpu.roll(tile(f + 5), 64, 1))
        dest[4] = tile(4)

    def unpack_pairs(source, f):
        return source[f] if f < 5 else pltpu.roll(source[f - 5], 64, 1)

    sub = iota((8, 128), 0)
    lo_lane = iota((8, 128), 1) < 64
    even = sub % 2 == 0

    def pack_rows_y(f, first_row):
        result = None
        for a in range(4):
            tile = tr[1, f, 8 * a : 8 * a + 8, :]
            shift = (2 * a - first_row) % 8
            moved = pltpu.roll(tile, shift, 0) if shift else tile
            result = moved if a == 0 else jnp.where(sub // 2 == a, moved, result)
        return result

    def pack_z(f, odd):
        strips = []
        for a in range(2):
            one = tr[2, f, 8 * a : 8 * a + 8, :]
            two = tr[2, f, 8 * a + 16 : 8 * a + 24, :]
            if odd:
                strips.append(jnp.where(even, pltpu.roll(two, 7, 0), one))
            else:
                strips.append(jnp.where(even, one, pltpu.roll(two, 1, 0)))
        keep = jnp.logical_not(lo_lane) if odd else lo_lane
        return jnp.where(keep, strips[0], pltpu.roll(strips[1], 64, 1))

    sends = (send_x, send_y, send_z)
    recvs = (recv_x, recv_y, recv_z)

    def copies(step):
        made = []
        for d in range(3):
            for way, target in ((0, up[d]), (1, down[d])):
                made.append(
                    pltpu.make_async_remote_copy(
                        src_ref=sends[d].at[way],
                        dst_ref=recvs[d].at[step, way],
                        send_sem=send_sem.at[step, 2 * d + way],
                        recv_sem=recv_sem.at[step, 2 * d + way],
                        device_id=target,
                        device_id_type=pl.DeviceIdType.MESH,
                    )
                )
        return made

    def sending(k):
        d, way = divmod(k, 2)
        return place[d] < count[d] - 1 if way == 0 else place[d] > 0

    def receiving(k):
        d, way = divmod(k, 2)
        return place[d] > 0 if way == 0 else place[d] < count[d] - 1

    def neighbours(step, d, f, a):
        tile = tr[d, f, 8 * a : 8 * a + 8, :]
        if d == 0:
            before = unpack_pairs(recv_x.at[step, 0], f) if a == 0 else tr[0, f, 8 * a - 8 : 8 * a, :]
            after = unpack_pairs(recv_x.at[step, 1], f) if a == 3 else tr[0, f, 8 * a + 8 : 8 * a + 16, :]
        elif d == 1:
            low = unpack_pairs(recv_y.at[step, 0], f)
            low = pltpu.roll(low, (8 - 2 * a) % 8, 0) if a else low
            before = jnp.where(sub < 2, low, pltpu.roll(tile, 2, 0))
            high = unpack_pairs(recv_y.at[step, 1], f)
            high = pltpu.roll(high, (6 - 2 * a) % 8, 0) if a < 3 else high
            after = jnp.where(sub >= 6, high, pltpu.roll(tile, 6, 0))
        else:
            low = recv_z[step, 0, f]
            high = recv_z[step, 1, f]
            if a % 2:
                low = pltpu.roll(low, 64, 1)
                high = pltpu.roll(high, 64, 1)
            if a < 2:
                low = pltpu.roll(low, 7, 0)
                high = pltpu.roll(high, 1, 0)
            before = jnp.where(even, low, pltpu.roll(tile, 1, 0))
            after = jnp.where(even, pltpu.roll(tile, 7, 0), high)
        return jnp.where(lo_lane, after, before)

    def corrections(step):
        sign = jnp.where(lo_lane, -1.0, 1.0)
        for d in range(3):
            for a in range(4):
                rows = slice(8 * a, 8 * a + 8)
                source = index[d, rows, :]
                w = [
                    jnp.take_along_axis(neighbours(step, d, f, a), source, axis=1) - tr[d, f, rows, :]
                    for f in range(FIELDS)
                ]
                inv, lam, mu, speed = [coef[i, rows, :] for i in range(4)]
                stiff = lam + 2.0 * mu
                if d == 0:
                    lam_v = lam * w[0]
                    flux = [inv * w[3], inv * w[6], inv * w[8], stiff * w[0], lam_v, lam_v,
                            mu * w[1], None, mu * w[2]]
                elif d == 1:
                    lam_v = lam * w[1]
                    flux = [inv * w[6], inv * w[4], inv * w[7], lam_v, stiff * w[1], lam_v,
                            mu * w[0], mu * w[2], None]
                else:
                    lam_v = lam * w[2]
                    flux = [inv * w[8], inv * w[7], inv * w[5], lam_v, lam_v, stiff * w[2],
                            None, mu * w[1], mu * w[0]]
                for f in range(FIELDS):
                    fixed = speed * w[f]
                    if flux[f] is not None:
                        fixed = fixed + sign * flux[f]
                    fixed = 0.5 * fixed
                    if d == 0:
                        cx[f, rows, :] = fixed
                    else:
                        tr[d, f, rows, :] = fixed
        for d in (1, 2):
            part = slice(128 * (d - 1), 128 * d)
            for f in range(FIELDS):
                ch[rows_of(f), part], cl[rows_of(f), part] = halves(tr[d, f])

    def step_body(step, carry):
        set_operand(q)
        advance(True, SERIES[1])
        advance(False, SERIES[2])
        for f in range(FIELDS):
            yh[hot_rows(f), :] = dot(hot_sel[...], xh[rows_of(f), :]).astype(BF16)
            yl[hot_rows(f), :] = dot(hot_sel[...], xl[rows_of(f), :]).astype(BF16)
            hot_sum[f] = jnp.zeros_like(hot_sum[f])

        def higher(k, c):
            weight = jnp.where(k == 0, SERIES[3], jnp.where(k == 1, SERIES[4], SERIES[5])).astype(F32)
            derive_hot()
            for j in range(4):
                part = slice(128 * j, 128 * (j + 1))
                for f, rate in enumerate(rates(part, hot_deriv, hot_rows, hot_coef)):
                    hot_sum[f, :, part] = hot_sum[f, :, part] + weight * rate
                    yh[hot_rows(f), part], yl[hot_rows(f), part] = halves(rate)
            return c

        lax.fori_loop(0, 3, higher, 0)
        for f in range(FIELDS):
            h, l = halves(hot_sum[f])
            full = acc[f] + (dot(hot_in_rows[...], h) + dot(hot_in_rows[...], l))
            acc[f] = full
            xh[rows_of(f), :], xl[rows_of(f), :] = halves(full)
            tr[0, f] = jnp.where(lane < 64, full[:, 0:128], full[:, 384:512])
        pack_pairs(lambda f: tr[0, f, 24:32, :], True, send_x.at[0])
        pack_pairs(lambda f: tr[0, f, 0:8, :], False, send_x.at[1])

        @pl.when(step == 0)
        def _():
            pl.semaphore_wait(barrier, 6)

        made = copies(step)

        def send(first, last):
            for k in range(first, last):

                @pl.when(sending(k))
                def _(k=k):
                    made[k].start()

        send(0, 2)
        faces = dot(xh[...], pick[...]) + dot(xl[...], pick[...])
        for f in range(FIELDS):
            tr[1, f] = faces[rows_of(f), 0:128]
            tr[2, f] = faces[rows_of(f), 128:256]
        pack_pairs(lambda f: pack_rows_y(f, 6), True, send_y.at[0])
        pack_pairs(lambda f: pack_rows_y(f, 0), False, send_y.at[1])
        for f in range(FIELDS):
            send_z[0, f] = pack_z(f, True)
            send_z[1, f] = pack_z(f, False)
        send(2, 6)
        derive()
        for k in range(6):

            @pl.when(receiving(k))
            def _(k=k):
                made[k].wait_recv()

        corrections(step)
        for j in range(4):
            part = slice(128 * j, 128 * (j + 1))
            for f, rate in enumerate(rates(part)):
                lifted = dot(ch[rows_of(f), :], lift[:, part]) + dot(cl[rows_of(f), :], lift[:, part])
                if j == 0:
                    lifted = lifted + jnp.where(lane < 64, cx[f], 0.0)
                if j == 3:
                    lifted = lifted + jnp.where(lane < 64, 0.0, cx[f])
                q[f, :, part] = q[f, :, part] + DT_STEP * (rate + LIFT_COEF * lifted)
        for k in range(6):

            @pl.when(sending(k))
            def _(k=k):
                made[k].wait_send()

        return carry

    lax.fori_loop(0, STEPS, step_body, 0)
    gather_out = (by_element[:, 10:11].astype(I32) == iota(square, 1)).astype(BF16)
    stores = [pltpu.make_async_copy(acc.at[f], out.at[f], small_sem.at[f]) for f in range(FIELDS)]
    for f in range(FIELDS):
        a, b, c = thirds(q[f])
        acc[f] = dot(gather_out, a) + dot(gather_out, b) + dot(gather_out, c)
        stores[f].start()
    for store in stores:
        store.wait()


def shards(
    wavefield, deriv_ops, density, lame_first, shear_modulus, high_order, element_cell, face_orient
):
    wave = jnp.swapaxes(wavefield[0, 0, 0], 0, 1)
    row = (1, ELEMENTS)
    any_space = pl.BlockSpec(memory_space=pl.ANY)
    field = (FIELDS, ELEMENTS, NODES)
    total = FIELDS * ELEMENTS
    result = pl.pallas_call(
        kernel,
        out_shape=jax.ShapeDtypeStruct(field, F32),
        in_specs=[any_space] * 8,
        out_specs=any_space,
        scratch_shapes=[
            pltpu.VMEM(field, F32),
            pltpu.VMEM(row, F32),
            pltpu.VMEM(row, F32),
            pltpu.VMEM(row, F32),
            pltpu.VMEM(row, I32),
            pltpu.VMEM(row, I32),
            pltpu.VMEM((6, 1, ELEMENTS), I32),
            pltpu.VMEM((3, NODES, NODES), F32),
            pltpu.VMEM((3, NODES, NODES), BF16),
            pltpu.VMEM((3, NODES, NODES), BF16),
            pltpu.VMEM((16, ELEMENTS), F32),
            pltpu.VMEM((4, ELEMENTS, 128), F32),
            pltpu.VMEM((3, ELEMENTS, 128), I32),
            pltpu.VMEM(field, F32),
            pltpu.VMEM(field, F32),
            pltpu.VMEM((total, NODES), BF16),
            pltpu.VMEM((total, NODES), BF16),
            pltpu.VMEM((3, 6 * ELEMENTS, NODES), F32),
            pltpu.VMEM((NODES, 256), BF16),
            pltpu.VMEM((256, NODES), BF16),
            pltpu.VMEM((3, FIELDS, ELEMENTS, 128), F32),
            pltpu.VMEM((total, 256), BF16),
            pltpu.VMEM((total, 256), BF16),
            pltpu.VMEM((FIELDS, ELEMENTS, 128), F32),
            pltpu.VMEM((ELEMENTS, HOT), BF16),
            pltpu.VMEM((3, HOT, 128), F32),
            pltpu.VMEM((FIELDS, HOT, NODES), F32),
            pltpu.VMEM((FIELDS * HOT, NODES), BF16),
            pltpu.VMEM((FIELDS * HOT, NODES), BF16),
            pltpu.VMEM((3, 6 * HOT, NODES), F32),
            pltpu.VMEM((HOT, ELEMENTS), BF16),
            pltpu.VMEM((2, 5, 8, 128), F32),
            pltpu.VMEM((2, 5, 8, 128), F32),
            pltpu.VMEM((2, FIELDS, 8, 128), F32),
            pltpu.VMEM((STEPS, 2, 5, 8, 128), F32),
            pltpu.VMEM((STEPS, 2, 5, 8, 128), F32),
            pltpu.VMEM((STEPS, 2, FIELDS, 8, 128), F32),
            pltpu.SemaphoreType.DMA((FIELDS,)),
            pltpu.SemaphoreType.DMA((3,)),
            pltpu.SemaphoreType.DMA((STEPS, 6)),
            pltpu.SemaphoreType.DMA((STEPS, 6)),
        ],
        compiler_params=pltpu.CompilerParams(
            collective_id=0, has_side_effects=True, vmem_limit_bytes=60 * 1024 * 1024
        ),
        name="elastic_steps",
    )(
        wave,
        deriv_ops,
        density.reshape(row),
        lame_first.reshape(row),
        shear_modulus.reshape(row),
        high_order.reshape(row),
        element_cell.reshape(row),
        face_orient.reshape(6, 1, ELEMENTS),
    )
    return jnp.swapaxes(result, 0, 1)[None, None, None]


def solution(mesh):
    row = P("gx", "gy", "ha", None)
    whole = P("gx", "gy", "ha", None, None, None)
    return jax.shard_map(
        shards,
        mesh=mesh,
        in_specs=(whole, P(), row, row, row, row, row, P("gx", "gy", "ha", None, None)),
        out_specs=whole,
        check_vma=False,
    )
```

```python
import math

import jax
import jax.numpy as jnp
from jax import lax
from jax.experimental import pallas as pl
from jax.experimental.pallas import tpu as pltpu
from jax.sharding import PartitionSpec as P

ELEMENTS = 32
HOT = 16
FIELDS = 9
NODES = 512
STEPS = 2
DT_STEP = 0.8
LIFT_COEF = 2.0
X_FIELDS = (0, 1, 2, 3, 6, 8)
Y_FIELDS = (0, 1, 2, 6, 4, 7)
Z_FIELDS = (0, 1, 2, 8, 7, 5)
AXIS_FIELDS = (X_FIELDS, Y_FIELDS, Z_FIELDS)
MESH_AXES = ("gx", "gy", "ha")
SERIES = tuple(DT_STEP**k / math.factorial(k + 1) for k in range(6))
F32 = jnp.float32
BF16 = jnp.bfloat16
I32 = jnp.int32
NT = (((1,), (1,)), ((), ()))
HIGHEST = lax.Precision.HIGHEST


def dot(a, b):
    return jnp.dot(a, b, preferred_element_type=F32)


def halves(value):
    high = value.astype(BF16)
    return high, (value - high.astype(F32)).astype(BF16)


def thirds(value):
    high = value.astype(BF16)
    rest = value - high.astype(F32)
    mid = rest.astype(BF16)
    return high, mid, (rest - mid.astype(F32)).astype(BF16)


def rows_of(field):
    return slice(ELEMENTS * field, ELEMENTS * (field + 1))


def iota(shape, dim):
    return lax.broadcasted_iota(I32, shape, dim)


def face_node(column):
    face = column // 64
    p = (column // 8) % 8
    r = column % 8
    far = 7 * (face % 2)
    return jnp.where(face < 2, p * 64 + far * 8 + r, p * 64 + r * 8 + far)


def restore(state, cell_in, out, cell, full, sems):
    load = pltpu.make_async_copy(cell_in, cell, sems.at[0])
    load.start()
    load.wait()
    square = (ELEMENTS, ELEMENTS)
    same = (iota(square, 0) == iota(square, 1)).astype(BF16)
    row = jnp.broadcast_to(cell[...], (8, ELEMENTS)).astype(BF16)
    column = lax.dot_general(same, row, NT, preferred_element_type=F32)[:, 0:1].astype(I32)
    gather_out = (column == iota(square, 1)).astype(BF16)
    stores = [pltpu.make_async_copy(full.at[f], out.at[f], sems.at[f]) for f in range(FIELDS)]
    for f in range(FIELDS):
        a, b, c = thirds(state[f])
        full[f] = dot(gather_out, a) + dot(gather_out, b) + dot(gather_out, c)
        stores[f].start()
    for store in stores:
        store.wait()


def kernel(
    wave_in, dops, dens_in, lame_in, shear_in, hot_in, cell_in, orient_in, q,
    wave, dens, lame, shear, hot, cell, orient,
    wf, wh, wl, small, coef, index, acc, xh, xl, deriv, pick, lift, tr, ch, cl, cx, spread,
    hot_in_rows, hot_coef, hot_sum, yh, yl, hot_deriv, hot_sel,
    send_x, send_y, send_z, recv_x, recv_y, recv_z, small_sem, load_sem, send_sem, recv_sem,
):
    barrier = pltpu.get_barrier_semaphore()
    place = [lax.axis_index(a) for a in MESH_AXES]
    count = [lax.axis_size(a) for a in MESH_AXES]
    up = [{a: lax.rem(i + 1, n)} for a, i, n in zip(MESH_AXES, place, count)]
    down = [{a: lax.rem(i + n - 1, n)} for a, i, n in zip(MESH_AXES, place, count)]
    arrivals = 0
    for d in range(3):
        for target, steps_left in ((up[d], count[d] - 1 - place[d]), (down[d], place[d])):

            @pl.when(steps_left > 0)
            def _(target=target):
                pl.semaphore_signal(barrier, 1, device_id=target, device_id_type=pl.DeviceIdType.MESH)

            arrivals = arrivals + lax.div(steps_left + count[d] - 1, count[d])

    small_loads = [
        pltpu.make_async_copy(source, dest, small_sem.at[i])
        for i, (source, dest) in enumerate(
            (
                (cell_in, cell), (hot_in, hot), (dens_in, dens), (lame_in, lame),
                (shear_in, shear), (orient_in, orient), (wave_in, wave),
            )
        )
    ]
    for load in small_loads:
        load.start()
    loads = [pltpu.make_async_copy(dops.at[a], wf.at[a], load_sem.at[a]) for a in range(3)]
    for load in loads:
        load.start()

    small[...] = jnp.zeros_like(small)
    for load in small_loads[:-1]:
        load.wait()
    small[0:1, :] = dens[...]
    small[1:2, :] = lame[...]
    small[2:3, :] = shear[...]
    small[3:4, :] = hot[...].astype(F32)
    for i in range(6):
        small[4 + i : 5 + i, :] = orient[i].astype(F32)
    small[10:11, :] = cell[...].astype(F32)
    square = (ELEMENTS, ELEMENTS)
    place_cell = (iota(square, 0) == jnp.broadcast_to(cell[...], square)).astype(F32)
    by_cell = lax.dot_general(place_cell, small[...], NT, precision=HIGHEST)
    wide = (ELEMENTS, 128)
    inv_rho = 1.0 / by_cell[:, 0:1]
    lame_col = by_cell[:, 1:2]
    shear_col = by_cell[:, 2:3]
    coef[0] = jnp.broadcast_to(inv_rho, wide)
    coef[1] = jnp.broadcast_to(lame_col, wide)
    coef[2] = jnp.broadcast_to(shear_col, wide)
    coef[3] = jnp.broadcast_to(jnp.sqrt((lame_col + 2.0 * shear_col) * inv_rho), wide)
    lane = iota(wide, 1)
    p_pos = (lane // 8) % 8
    r_pos = lane % 8
    for d in range(3):
        low = jnp.broadcast_to(by_cell[:, 4 + 2 * d : 5 + 2 * d], wide)
        high = jnp.broadcast_to(by_cell[:, 5 + 2 * d : 6 + 2 * d], wide)
        code = jnp.where(lane < 64, low, high).astype(I32)
        p_src = jnp.where((code & 1) != 0, 7 - p_pos, p_pos)
        r_src = jnp.where((code & 2) != 0, 7 - r_pos, r_pos)
        node = jnp.where((code & 4) != 0, r_src * 8 + p_src, p_src * 8 + r_src)
        index[d] = node + jnp.where(lane < 64, 64, 0)
    pick[...] = (iota((NODES, 256), 0) == face_node(iota((NODES, 256), 1))).astype(BF16)
    lift[...] = (iota((256, NODES), 1) == face_node(iota((256, NODES), 0))).astype(BF16)
    slots = (HOT, ELEMENTS)
    flag_row = lax.dot_general(small[...], place_cell, NT, precision=HIGHEST)[3:4, :]
    upto = (iota(square, 0) <= iota(square, 1)).astype(F32)
    rank_row = lax.dot_general(
        jnp.broadcast_to(flag_row, (8, ELEMENTS)), upto, (((1,), (0,)), ((), ())), precision=HIGHEST
    )[0:1, :].astype(I32)
    chosen = (iota(slots, 0) + 1 == jnp.broadcast_to(rank_row, slots)) & (
        jnp.broadcast_to(flag_row, slots) > 0.5
    )
    select = chosen.astype(F32)
    hot_sel[...] = select.astype(BF16)
    of_slot = lax.dot_general(select, by_cell, (((1,), (0,)), ((), ())), precision=HIGHEST)
    filled = of_slot[:, 0:1] > 0.0
    hot_coef[0] = jnp.broadcast_to(
        jnp.where(filled, 1.0 / jnp.where(filled, of_slot[:, 0:1], 1.0), 0.0), (HOT, 128)
    )
    hot_coef[1] = jnp.broadcast_to(of_slot[:, 1:2], (HOT, 128))
    hot_coef[2] = jnp.broadcast_to(of_slot[:, 2:3], (HOT, 128))
    slot_col = iota((ELEMENTS, HOT), 1) + 1
    below = (iota(square, 1) <= iota(square, 0)).astype(F32)
    rank_col = lax.dot_general(
        below, jnp.broadcast_to(by_cell[:, 3:4], (ELEMENTS, 8)), (((1,), (0,)), ((), ())), precision=HIGHEST
    )[:, 0:1]
    back = (slot_col == rank_col.astype(I32)) & (by_cell[:, 3:4] > 0.5)
    hot_in_rows[...] = back.astype(BF16)
    gather_in = place_cell.astype(BF16)
    small_loads[-1].wait()
    for f in range(FIELDS):
        a, b, c = thirds(wave[f])
        full = dot(gather_in, a) + dot(gather_in, b) + dot(gather_in, c)
        q[f] = full
        xh[rows_of(f), :], xl[rows_of(f), :] = halves(full)

    for a in range(3):
        loads[a].wait()

        def split(i, carry, a=a):
            part = pl.ds(pl.multiple_of(i * 64, 64), 64)
            h, l = halves(wf[a, part, :])
            wh[a, part, :] = h
            wl[a, part, :] = l
            return carry

        lax.fori_loop(0, NODES // 64, split, 0)

    for recv, at, n in zip((recv_x, recv_y, recv_z), place, count):
        for edge, slot in ((0, 0), (n - 1, 1)):

            @pl.when(at == edge)
            def _(recv=recv, slot=slot):
                for s in range(STEPS):
                    recv[s, slot] = jnp.zeros_like(recv[s, slot])

    def derive():
        for a, fields in enumerate(AXIS_FIELDS):
            h = jnp.concatenate([xh[rows_of(f), :] for f in fields], axis=0)
            l = jnp.concatenate([xl[rows_of(f), :] for f in fields], axis=0)
            deriv[a] = dot(h, wh[a]) + dot(l, wh[a]) + dot(h, wl[a])

    def hot_rows(field):
        return slice(HOT * field, HOT * (field + 1))

    def derive_hot():
        for a, fields in enumerate(AXIS_FIELDS):
            h = [yh[hot_rows(f), :] for f in fields]
            l = [yl[hot_rows(f), :] for f in fields]
            both = dot(jnp.concatenate(h + l, axis=0), wh[a])
            cross = dot(jnp.concatenate(h, axis=0), wl[a])
            hot_deriv[a] = both[0 : 6 * HOT] + (both[6 * HOT :] + cross)

    def rates(part, source=deriv, rows=rows_of, factors=coef):
        x = [source[0, rows(i), part] for i in range(6)]
        y = [source[1, rows(i), part] for i in range(6)]
        z = [source[2, rows(i), part] for i in range(6)]
        inv, lam, mu = factors[0], factors[1], factors[2]
        lam_div = lam * (x[0] + y[1] + z[2])
        mu2 = 2.0 * mu
        return [
            inv * (x[3] + y[3] + z[3]),
            inv * (x[4] + y[4] + z[4]),
            inv * (x[5] + y[5] + z[5]),
            lam_div + mu2 * x[0],
            lam_div + mu2 * y[1],
            lam_div + mu2 * z[2],
            mu * (x[1] + y[0]),
            mu * (y[2] + z[1]),
            mu * (x[2] + z[0]),
        ]

    def advance(first, weight):
        derive()
        for j in range(4):
            part = slice(128 * j, 128 * (j + 1))
            for f, rate in enumerate(rates(part)):
                term = weight * rate
                base = q if first else acc
                acc[f, :, part] = base[f, :, part] + term
                xh[rows_of(f), part], xl[rows_of(f), part] = halves(rate)

    def pack_pairs(tile, upper, dest):
        keep = (iota((8, 128), 1) >= 64) if upper else (iota((8, 128), 1) < 64)
        for f in range(4):
            dest[f] = jnp.where(keep, tile(f), pltpu.roll(tile(f + 5), 64, 1))
        dest[4] = tile(4)

    def unpack_pairs(source, f):
        return source[f] if f < 5 else pltpu.roll(source[f - 5], 64, 1)

    sub = iota((8, 128), 0)
    lo_lane = iota((8, 128), 1) < 64
    even = sub % 2 == 0

    def pack_rows_y(f, first_row):
        result = None
        for a in range(4):
            tile = tr[1, f, 8 * a : 8 * a + 8, :]
            shift = (2 * a - first_row) % 8
            moved = pltpu.roll(tile, shift, 0) if shift else tile
            result = moved if a == 0 else jnp.where(sub // 2 == a, moved, result)
        return result

    def pack_z(f, odd):
        strips = []
        for a in range(2):
            one = tr[2, f, 8 * a : 8 * a + 8, :]
            two = tr[2, f, 8 * a + 16 : 8 * a + 24, :]
            if odd:
                strips.append(jnp.where(even, pltpu.roll(two, 7, 0), one))
            else:
                strips.append(jnp.where(even, one, pltpu.roll(two, 1, 0)))
        keep = jnp.logical_not(lo_lane) if odd else lo_lane
        return jnp.where(keep, strips[0], pltpu.roll(strips[1], 64, 1))

    sends = (send_x, send_y, send_z)
    recvs = (recv_x, recv_y, recv_z)

    def copies(step):
        made = []
        for d in range(3):
            for way, target in ((0, up[d]), (1, down[d])):
                made.append(
                    pltpu.make_async_remote_copy(
                        src_ref=sends[d].at[way],
                        dst_ref=recvs[d].at[step, way],
                        send_sem=send_sem.at[step, 2 * d + way],
                        recv_sem=recv_sem.at[step, 2 * d + way],
                        device_id=target,
                        device_id_type=pl.DeviceIdType.MESH,
                    )
                )
        return made

    def sending(k):
        d, way = divmod(k, 2)
        return place[d] < count[d] - 1 if way == 0 else place[d] > 0

    def receiving(k):
        d, way = divmod(k, 2)
        return place[d] > 0 if way == 0 else place[d] < count[d] - 1

    def neighbours(step, d, f, a):
        tile = tr[d, f, 8 * a : 8 * a + 8, :]
        if d == 0:
            before = unpack_pairs(recv_x.at[step, 0], f) if a == 0 else tr[0, f, 8 * a - 8 : 8 * a, :]
            after = unpack_pairs(recv_x.at[step, 1], f) if a == 3 else tr[0, f, 8 * a + 8 : 8 * a + 16, :]
        elif d == 1:
            low = unpack_pairs(recv_y.at[step, 0], f)
            low = pltpu.roll(low, (8 - 2 * a) % 8, 0) if a else low
            before = jnp.where(sub < 2, low, pltpu.roll(tile, 2, 0))
            high = unpack_pairs(recv_y.at[step, 1], f)
            high = pltpu.roll(high, (6 - 2 * a) % 8, 0) if a < 3 else high
            after = jnp.where(sub >= 6, high, pltpu.roll(tile, 6, 0))
        else:
            low = recv_z[step, 0, f]
            high = recv_z[step, 1, f]
            if a % 2:
                low = pltpu.roll(low, 64, 1)
                high = pltpu.roll(high, 64, 1)
            if a < 2:
                low = pltpu.roll(low, 7, 0)
                high = pltpu.roll(high, 1, 0)
            before = jnp.where(even, low, pltpu.roll(tile, 1, 0))
            after = jnp.where(even, pltpu.roll(tile, 7, 0), high)
        return jnp.where(lo_lane, after, before)

    def corrections(step, d):
        sign = jnp.where(lo_lane, -1.0, 1.0)
        for a in range(4):
            rows = slice(8 * a, 8 * a + 8)
            source = index[d, rows, :]
            w = [
                jnp.take_along_axis(neighbours(step, d, f, a), source, axis=1) - tr[d, f, rows, :]
                for f in range(FIELDS)
            ]
            inv, lam, mu, speed = [coef[i, rows, :] for i in range(4)]
            stiff = lam + 2.0 * mu
            if d == 0:
                lam_v = lam * w[0]
                flux = [inv * w[3], inv * w[6], inv * w[8], stiff * w[0], lam_v, lam_v,
                        mu * w[1], None, mu * w[2]]
            elif d == 1:
                lam_v = lam * w[1]
                flux = [inv * w[6], inv * w[4], inv * w[7], lam_v, stiff * w[1], lam_v,
                        mu * w[0], mu * w[2], None]
            else:
                lam_v = lam * w[2]
                flux = [inv * w[8], inv * w[7], inv * w[5], lam_v, lam_v, stiff * w[2],
                        None, mu * w[1], mu * w[0]]
            for f in range(FIELDS):
                fixed = speed * w[f]
                if flux[f] is not None:
                    fixed = fixed + sign * flux[f]
                fixed = 0.5 * fixed
                if d == 0:
                    cx[f, rows, :] = fixed
                else:
                    tr[d, f, rows, :] = fixed
        if d:
            part = slice(128 * (d - 1), 128 * d)
            for f in range(FIELDS):
                ch[rows_of(f), part], cl[rows_of(f), part] = halves(tr[d, f])

    def step_body(step, carry):
        advance(True, SERIES[1])
        advance(False, SERIES[2])
        for f in range(FIELDS):
            yh[hot_rows(f), :] = dot(hot_sel[...], xh[rows_of(f), :]).astype(BF16)
            yl[hot_rows(f), :] = dot(hot_sel[...], xl[rows_of(f), :]).astype(BF16)
            hot_sum[f] = jnp.zeros_like(hot_sum[f])

        def higher(k, c):
            weight = jnp.where(k == 0, SERIES[3], jnp.where(k == 1, SERIES[4], SERIES[5])).astype(F32)
            derive_hot()
            for j in range(4):
                part = slice(128 * j, 128 * (j + 1))
                for f, rate in enumerate(rates(part, hot_deriv, hot_rows, hot_coef)):
                    hot_sum[f, :, part] = hot_sum[f, :, part] + weight * rate
                    yh[hot_rows(f), part], yl[hot_rows(f), part] = halves(rate)
            return c

        lax.fori_loop(0, 3, higher, 0)
        for f in range(FIELDS):
            h, l = halves(hot_sum[f])
            full = acc[f] + (dot(hot_in_rows[...], h) + dot(hot_in_rows[...], l))
            acc[f] = full
            xh[rows_of(f), :], xl[rows_of(f), :] = halves(full)
            tr[0, f] = jnp.where(lane < 64, full[:, 0:128], full[:, 384:512])
        pack_pairs(lambda f: tr[0, f, 24:32, :], True, send_x.at[0])
        pack_pairs(lambda f: tr[0, f, 0:8, :], False, send_x.at[1])

        @pl.when(step == 0)
        def _():
            pl.semaphore_wait(barrier, arrivals)

        made = copies(step)

        def send(d):
            for k in (2 * d, 2 * d + 1):

                @pl.when(sending(k))
                def _(k=k):
                    made[k].start()

        send(0)
        faces = dot(xh[...], pick[...]) + dot(xl[...], pick[...])
        for f in range(FIELDS):
            tr[1, f] = faces[rows_of(f), 0:128]
            tr[2, f] = faces[rows_of(f), 128:256]
        for f in range(FIELDS):
            send_z[0, f] = pack_z(f, True)
            send_z[1, f] = pack_z(f, False)
        send(2)
        pack_pairs(lambda f: pack_rows_y(f, 6), True, send_y.at[0])
        pack_pairs(lambda f: pack_rows_y(f, 0), False, send_y.at[1])
        send(1)
        derive()
        for j in range(4):
            part = slice(128 * j, 128 * (j + 1))
            for f, rate in enumerate(rates(part)):
                acc[f, :, part] = q[f, :, part] + DT_STEP * rate

        def receive(d):
            for k in (2 * d, 2 * d + 1):

                @pl.when(receiving(k))
                def _(k=k):
                    made[k].wait_recv()

        receive(2)
        corrections(step, 2)
        receive(1)
        corrections(step, 1)
        spread[...] = dot(ch[...], lift[...]) + dot(cl[...], lift[...])
        for f in range(FIELDS):
            for j in range(4):
                part = slice(128 * j, 128 * (j + 1))
                full = acc[f, :, part] + (DT_STEP * LIFT_COEF) * spread[rows_of(f), part]
                if j in (1, 2):
                    q[f, :, part] = full
                    xh[rows_of(f), part], xl[rows_of(f), part] = halves(full)
                else:
                    acc[f, :, part] = full
        receive(0)
        corrections(step, 0)
        for f in range(FIELDS):
            for j, mine in ((0, lane < 64), (3, lane >= 64)):
                part = slice(128 * j, 128 * (j + 1))
                full = acc[f, :, part] + jnp.where(mine, (DT_STEP * LIFT_COEF) * cx[f], 0.0)
                q[f, :, part] = full
                xh[rows_of(f), part], xl[rows_of(f), part] = halves(full)
        for k in range(6):

            @pl.when(sending(k))
            def _(k=k):
                made[k].wait_send()

        return carry

    lax.fori_loop(0, STEPS, step_body, 0)


def shards(
    wavefield, deriv_ops, density, lame_first, shear_modulus, high_order, element_cell, face_orient
):
    wave = jnp.swapaxes(wavefield[0, 0, 0], 0, 1)
    row = (1, ELEMENTS)
    any_space = pl.BlockSpec(memory_space=pltpu.HBM)
    field = (FIELDS, ELEMENTS, NODES)
    total = FIELDS * ELEMENTS
    result = pl.pallas_call(
        kernel,
        out_shape=jax.ShapeDtypeStruct(field, F32),
        in_specs=[any_space] * 8,
        out_specs=pl.BlockSpec(memory_space=pltpu.VMEM),
        scratch_shapes=[
            pltpu.VMEM(field, F32),
            pltpu.VMEM(row, F32),
            pltpu.VMEM(row, F32),
            pltpu.VMEM(row, F32),
            pltpu.VMEM(row, I32),
            pltpu.VMEM(row, I32),
            pltpu.VMEM((6, 1, ELEMENTS), I32),
            pltpu.VMEM((3, NODES, NODES), F32),
            pltpu.VMEM((3, NODES, NODES), BF16),
            pltpu.VMEM((3, NODES, NODES), BF16),
            pltpu.VMEM((16, ELEMENTS), F32),
            pltpu.VMEM((4, ELEMENTS, 128), F32),
            pltpu.VMEM((3, ELEMENTS, 128), I32),
            pltpu.VMEM(field, F32),
            pltpu.VMEM((total, NODES), BF16),
            pltpu.VMEM((total, NODES), BF16),
            pltpu.VMEM((3, 6 * ELEMENTS, NODES), F32),
            pltpu.VMEM((NODES, 256), BF16),
            pltpu.VMEM((256, NODES), BF16),
            pltpu.VMEM((3, FIELDS, ELEMENTS, 128), F32),
            pltpu.VMEM((total, 256), BF16),
            pltpu.VMEM((total, 256), BF16),
            pltpu.VMEM((FIELDS, ELEMENTS, 128), F32),
            pltpu.VMEM((total, NODES), F32),
            pltpu.VMEM((ELEMENTS, HOT), BF16),
            pltpu.VMEM((3, HOT, 128), F32),
            pltpu.VMEM((FIELDS, HOT, NODES), F32),
            pltpu.VMEM((FIELDS * HOT, NODES), BF16),
            pltpu.VMEM((FIELDS * HOT, NODES), BF16),
            pltpu.VMEM((3, 6 * HOT, NODES), F32),
            pltpu.VMEM((HOT, ELEMENTS), BF16),
            pltpu.VMEM((2, 5, 8, 128), F32),
            pltpu.VMEM((2, 5, 8, 128), F32),
            pltpu.VMEM((2, FIELDS, 8, 128), F32),
            pltpu.VMEM((STEPS, 2, 5, 8, 128), F32),
            pltpu.VMEM((STEPS, 2, 5, 8, 128), F32),
            pltpu.VMEM((STEPS, 2, FIELDS, 8, 128), F32),
            pltpu.SemaphoreType.DMA((FIELDS,)),
            pltpu.SemaphoreType.DMA((3,)),
            pltpu.SemaphoreType.DMA((STEPS, 6)),
            pltpu.SemaphoreType.DMA((STEPS, 6)),
        ],
        compiler_params=pltpu.CompilerParams(
            collective_id=0, has_side_effects=True, vmem_limit_bytes=24 * 1024 * 1024
        ),
        name="elastic_steps",
    )(
        *(
            pltpu.with_memory_space_constraint(x, pltpu.HBM)
            for x in (
                wave,
                deriv_ops,
                density.reshape(row),
                lame_first.reshape(row),
                shear_modulus.reshape(row),
                high_order.reshape(row),
                element_cell.reshape(row),
                face_orient.reshape(6, 1, ELEMENTS),
            )
        ),
    )
    vmem = pl.BlockSpec(memory_space=pltpu.VMEM)
    result = pl.pallas_call(
        restore,
        out_shape=jax.ShapeDtypeStruct(field, F32),
        in_specs=[vmem, any_space],
        out_specs=any_space,
        scratch_shapes=[pltpu.VMEM(row, I32), pltpu.VMEM(field, F32), pltpu.SemaphoreType.DMA((FIELDS,))],
        compiler_params=pltpu.CompilerParams(vmem_limit_bytes=8 * 1024 * 1024),
        name="restore",
    )(result, element_cell.reshape(row))
    return jnp.swapaxes(result, 0, 1)[None, None, None]


def solution(mesh):
    row = P("gx", "gy", "ha", None)
    whole = P("gx", "gy", "ha", None, None, None)
    return jax.shard_map(
        shards,
        mesh=mesh,
        in_specs=(whole, P(), row, row, row, row, row, P("gx", "gy", "ha", None, None)),
        out_specs=whole,
        check_vma=False,
    )
```

```python
import math

import jax
import jax.numpy as jnp
from jax import lax
from jax.experimental import pallas as pl
from jax.experimental.pallas import tpu as pltpu
from jax.sharding import PartitionSpec as P

ELEMENTS = 32
HOT = 16
FIELDS = 9
NODES = 512
STEPS = 2
DT_STEP = 0.8
LIFT_COEF = 2.0
X_FIELDS = (0, 1, 2, 3, 6, 8)
Y_FIELDS = (0, 1, 2, 6, 4, 7)
Z_FIELDS = (0, 1, 2, 8, 7, 5)
AXIS_FIELDS = (X_FIELDS, Y_FIELDS, Z_FIELDS)
MESH_AXES = ("gx", "gy", "ha")
SERIES = tuple(DT_STEP**k / math.factorial(k + 1) for k in range(6))
F32 = jnp.float32
BF16 = jnp.bfloat16
I32 = jnp.int32
NT = (((1,), (1,)), ((), ()))
HIGHEST = lax.Precision.HIGHEST


def dot(a, b):
    return jnp.dot(a, b, preferred_element_type=F32)


def halves(value):
    high = value.astype(BF16)
    return high, (value - high.astype(F32)).astype(BF16)


def thirds(value):
    high = value.astype(BF16)
    rest = value - high.astype(F32)
    mid = rest.astype(BF16)
    return high, mid, (rest - mid.astype(F32)).astype(BF16)


def rows_of(field):
    return slice(ELEMENTS * field, ELEMENTS * (field + 1))


def iota(shape, dim):
    return lax.broadcasted_iota(I32, shape, dim)


def face_node(column):
    face = column // 64
    p = (column // 8) % 8
    r = column % 8
    far = 7 * (face % 2)
    return jnp.where(face < 2, p * 64 + far * 8 + r, p * 64 + r * 8 + far)


def restore(state, gather, out, full, sems):
    stores = [pltpu.make_async_copy(full.at[f], out.at[f], sems.at[f]) for f in range(FIELDS)]
    gather_out = gather[...].astype(BF16)
    for f in range(FIELDS):
        a, b, c = thirds(state[f])
        full[f] = dot(gather_out, a) + dot(gather_out, b) + dot(gather_out, c)
        stores[f].start()
    for store in stores:
        store.wait()


def kernel(
    wave_in, dops, dens_in, lame_in, shear_in, hot_in, cell_in, orient_in, q, gather_out,
    wave, dens, lame, shear, hot, cell, orient,
    wf, wh, wl, small, coef, index, acc, xh, xl, deriv, pick, lift, tr, ch, cl, cx, spread,
    hot_in_rows, hot_coef, hot_sum, yh, yl, hot_deriv, hot_sel,
    send_x, send_y, send_z, recv_x, recv_y, recv_z, small_sem, load_sem, send_sem, recv_sem,
):
    barrier = pltpu.get_barrier_semaphore()
    place = [lax.axis_index(a) for a in MESH_AXES]
    count = [lax.axis_size(a) for a in MESH_AXES]
    up = [{a: lax.rem(i + 1, n)} for a, i, n in zip(MESH_AXES, place, count)]
    down = [{a: lax.rem(i + n - 1, n)} for a, i, n in zip(MESH_AXES, place, count)]
    small_loads = [
        pltpu.make_async_copy(source, dest, small_sem.at[i])
        for i, (source, dest) in enumerate(
            (
                (cell_in, cell), (hot_in, hot), (dens_in, dens), (lame_in, lame),
                (shear_in, shear), (orient_in, orient), (wave_in, wave),
            )
        )
    ]
    for load in small_loads:
        load.start()
    loads = [pltpu.make_async_copy(dops.at[a], wf.at[a], load_sem.at[a]) for a in range(3)]
    for load in loads:
        load.start()

    arrivals = 0
    for d in range(3):
        for target, steps_left in ((up[d], count[d] - 1 - place[d]), (down[d], place[d])):

            @pl.when(steps_left > 0)
            def _(target=target):
                pl.semaphore_signal(barrier, 1, device_id=target, device_id_type=pl.DeviceIdType.MESH)

            arrivals = arrivals + lax.div(steps_left + count[d] - 1, count[d])

    pick[...] = (iota((NODES, 256), 0) == face_node(iota((NODES, 256), 1))).astype(BF16)
    lift[...] = (iota((256, NODES), 1) == face_node(iota((256, NODES), 0))).astype(BF16)

    for recv, at, n in zip((recv_x, recv_y, recv_z), place, count):
        for edge, slot in ((0, 0), (n - 1, 1)):

            @pl.when(at == edge)
            def _(recv=recv, slot=slot):
                for s in range(STEPS):
                    recv[s, slot] = jnp.zeros_like(recv[s, slot])

    def derive():
        for a, fields in enumerate(AXIS_FIELDS):
            h = jnp.concatenate([xh[rows_of(f), :] for f in fields], axis=0)
            l = jnp.concatenate([xl[rows_of(f), :] for f in fields], axis=0)
            deriv[a] = dot(h, wh[a]) + dot(l, wh[a]) + dot(h, wl[a])

    small[...] = jnp.zeros_like(small)
    for load in small_loads[:-1]:
        load.wait()
    small[0:1, :] = dens[...]
    small[1:2, :] = lame[...]
    small[2:3, :] = shear[...]
    small[3:4, :] = hot[...].astype(F32)
    for i in range(6):
        small[4 + i : 5 + i, :] = orient[i].astype(F32)
    small[10:11, :] = cell[...].astype(F32)
    square = (ELEMENTS, ELEMENTS)
    place_cell = (iota(square, 0) == jnp.broadcast_to(cell[...], square)).astype(F32)
    same = (iota(square, 0) == iota(square, 1)).astype(BF16)
    cell_row = jnp.broadcast_to(cell[...], (8, ELEMENTS)).astype(F32).astype(BF16)
    cell_col = lax.dot_general(same, cell_row, NT, preferred_element_type=F32)[:, 0:1]
    gather_out[...] = (cell_col.astype(I32) == iota(square, 1)).astype(F32)
    by_cell = lax.dot_general(place_cell, small[...], NT, precision=HIGHEST)
    wide = (ELEMENTS, 128)
    inv_rho = 1.0 / by_cell[:, 0:1]
    lame_col = by_cell[:, 1:2]
    shear_col = by_cell[:, 2:3]
    coef[0] = jnp.broadcast_to(inv_rho, wide)
    coef[1] = jnp.broadcast_to(lame_col, wide)
    coef[2] = jnp.broadcast_to(shear_col, wide)
    coef[3] = jnp.broadcast_to(jnp.sqrt((lame_col + 2.0 * shear_col) * inv_rho), wide)
    lane = iota(wide, 1)
    p_pos = (lane // 8) % 8
    r_pos = lane % 8
    for d in range(3):
        low = jnp.broadcast_to(by_cell[:, 4 + 2 * d : 5 + 2 * d], wide)
        high = jnp.broadcast_to(by_cell[:, 5 + 2 * d : 6 + 2 * d], wide)
        code = jnp.where(lane < 64, low, high).astype(I32)
        p_src = jnp.where((code & 1) != 0, 7 - p_pos, p_pos)
        r_src = jnp.where((code & 2) != 0, 7 - r_pos, r_pos)
        node = jnp.where((code & 4) != 0, r_src * 8 + p_src, p_src * 8 + r_src)
        index[d] = node + jnp.where(lane < 64, 64, 0)
    slots = (HOT, ELEMENTS)
    flag_row = lax.dot_general(small[...], place_cell, NT, precision=HIGHEST)[3:4, :]
    upto = (iota(square, 0) <= iota(square, 1)).astype(F32)
    rank_row = lax.dot_general(
        jnp.broadcast_to(flag_row, (8, ELEMENTS)), upto, (((1,), (0,)), ((), ())), precision=HIGHEST
    )[0:1, :].astype(I32)
    chosen = (iota(slots, 0) + 1 == jnp.broadcast_to(rank_row, slots)) & (
        jnp.broadcast_to(flag_row, slots) > 0.5
    )
    select = chosen.astype(F32)
    hot_sel[...] = select.astype(BF16)
    of_slot = lax.dot_general(select, by_cell, (((1,), (0,)), ((), ())), precision=HIGHEST)
    filled = of_slot[:, 0:1] > 0.0
    hot_coef[0] = jnp.broadcast_to(
        jnp.where(filled, 1.0 / jnp.where(filled, of_slot[:, 0:1], 1.0), 0.0), (HOT, 128)
    )
    hot_coef[1] = jnp.broadcast_to(of_slot[:, 1:2], (HOT, 128))
    hot_coef[2] = jnp.broadcast_to(of_slot[:, 2:3], (HOT, 128))
    slot_col = iota((ELEMENTS, HOT), 1) + 1
    below = (iota(square, 1) <= iota(square, 0)).astype(F32)
    rank_col = lax.dot_general(
        below, jnp.broadcast_to(by_cell[:, 3:4], (ELEMENTS, 8)), (((1,), (0,)), ((), ())), precision=HIGHEST
    )[:, 0:1]
    back = (slot_col == rank_col.astype(I32)) & (by_cell[:, 3:4] > 0.5)
    hot_in_rows[...] = back.astype(BF16)
    gather_in = place_cell.astype(BF16)
    small_loads[-1].wait()
    for f in range(FIELDS):
        a, b, c = thirds(wave[f])
        full = dot(gather_in, a) + dot(gather_in, b) + dot(gather_in, c)
        q[f] = full
        xh[rows_of(f), :], xl[rows_of(f), :] = halves(full)

    for a in range(3):
        loads[a].wait()

        def split(i, carry, a=a):
            part = pl.ds(pl.multiple_of(i * 64, 64), 64)
            h, l = halves(wf[a, part, :])
            wh[a, part, :] = h
            wl[a, part, :] = l
            return carry

        lax.fori_loop(0, NODES // 64, split, 0)

    def hot_rows(field):
        return slice(HOT * field, HOT * (field + 1))

    def derive_hot():
        for a, fields in enumerate(AXIS_FIELDS):
            h = [yh[hot_rows(f), :] for f in fields]
            l = [yl[hot_rows(f), :] for f in fields]
            both = dot(jnp.concatenate(h + l, axis=0), wh[a])
            cross = dot(jnp.concatenate(h, axis=0), wl[a])
            hot_deriv[a] = both[0 : 6 * HOT] + (both[6 * HOT :] + cross)

    def rates(part, source=deriv, rows=rows_of, factors=coef):
        x = [source[0, rows(i), part] for i in range(6)]
        y = [source[1, rows(i), part] for i in range(6)]
        z = [source[2, rows(i), part] for i in range(6)]
        inv, lam, mu = factors[0], factors[1], factors[2]
        lam_div = lam * (x[0] + y[1] + z[2])
        mu2 = 2.0 * mu
        return [
            inv * (x[3] + y[3] + z[3]),
            inv * (x[4] + y[4] + z[4]),
            inv * (x[5] + y[5] + z[5]),
            lam_div + mu2 * x[0],
            lam_div + mu2 * y[1],
            lam_div + mu2 * z[2],
            mu * (x[1] + y[0]),
            mu * (y[2] + z[1]),
            mu * (x[2] + z[0]),
        ]

    def advance(first, weight):
        derive()
        for j in range(4):
            part = slice(128 * j, 128 * (j + 1))
            for f, rate in enumerate(rates(part)):
                term = weight * rate
                base = q if first else acc
                acc[f, :, part] = base[f, :, part] + term
                xh[rows_of(f), part], xl[rows_of(f), part] = halves(rate)

    def pack_pairs(tile, upper, dest):
        keep = (iota((8, 128), 1) >= 64) if upper else (iota((8, 128), 1) < 64)
        for f in range(4):
            dest[f] = jnp.where(keep, tile(f), pltpu.roll(tile(f + 5), 64, 1))
        dest[4] = tile(4)

    def unpack_pairs(source, f):
        return source[f] if f < 5 else pltpu.roll(source[f - 5], 64, 1)

    sub = iota((8, 128), 0)
    lo_lane = iota((8, 128), 1) < 64
    even = sub % 2 == 0

    def pack_rows_y(f, first_row):
        result = None
        for a in range(4):
            tile = tr[1, f, 8 * a : 8 * a + 8, :]
            shift = (2 * a - first_row) % 8
            moved = pltpu.roll(tile, shift, 0) if shift else tile
            result = moved if a == 0 else jnp.where(sub // 2 == a, moved, result)
        return result

    def pack_z(f, odd):
        strips = []
        for a in range(2):
            one = tr[2, f, 8 * a : 8 * a + 8, :]
            two = tr[2, f, 8 * a + 16 : 8 * a + 24, :]
            if odd:
                strips.append(jnp.where(even, pltpu.roll(two, 7, 0), one))
            else:
                strips.append(jnp.where(even, one, pltpu.roll(two, 1, 0)))
        keep = jnp.logical_not(lo_lane) if odd else lo_lane
        return jnp.where(keep, strips[0], pltpu.roll(strips[1], 64, 1))

    sends = (send_x, send_y, send_z)
    recvs = (recv_x, recv_y, recv_z)

    def copies(step):
        made = []
        for d in range(3):
            for way, target in ((0, up[d]), (1, down[d])):
                made.append(
                    pltpu.make_async_remote_copy(
                        src_ref=sends[d].at[way],
                        dst_ref=recvs[d].at[step, way],
                        send_sem=send_sem.at[step, 2 * d + way],
                        recv_sem=recv_sem.at[step, 2 * d + way],
                        device_id=target,
                        device_id_type=pl.DeviceIdType.MESH,
                    )
                )
        return made

    def sending(k):
        d, way = divmod(k, 2)
        return place[d] < count[d] - 1 if way == 0 else place[d] > 0

    def receiving(k):
        d, way = divmod(k, 2)
        return place[d] > 0 if way == 0 else place[d] < count[d] - 1

    def neighbours(step, d, f, a):
        tile = tr[d, f, 8 * a : 8 * a + 8, :]
        if d == 0:
            before = unpack_pairs(recv_x.at[step, 0], f) if a == 0 else tr[0, f, 8 * a - 8 : 8 * a, :]
            after = unpack_pairs(recv_x.at[step, 1], f) if a == 3 else tr[0, f, 8 * a + 8 : 8 * a + 16, :]
        elif d == 1:
            low = unpack_pairs(recv_y.at[step, 0], f)
            low = pltpu.roll(low, (8 - 2 * a) % 8, 0) if a else low
            before = jnp.where(sub < 2, low, pltpu.roll(tile, 2, 0))
            high = unpack_pairs(recv_y.at[step, 1], f)
            high = pltpu.roll(high, (6 - 2 * a) % 8, 0) if a < 3 else high
            after = jnp.where(sub >= 6, high, pltpu.roll(tile, 6, 0))
        else:
            low = recv_z[step, 0, f]
            high = recv_z[step, 1, f]
            if a % 2:
                low = pltpu.roll(low, 64, 1)
                high = pltpu.roll(high, 64, 1)
            if a < 2:
                low = pltpu.roll(low, 7, 0)
                high = pltpu.roll(high, 1, 0)
            before = jnp.where(even, low, pltpu.roll(tile, 1, 0))
            after = jnp.where(even, pltpu.roll(tile, 7, 0), high)
        return jnp.where(lo_lane, after, before)

    def corrections(step, d):
        sign = jnp.where(lo_lane, -1.0, 1.0)
        for a in range(4):
            rows = slice(8 * a, 8 * a + 8)
            source = index[d, rows, :]
            w = [
                jnp.take_along_axis(neighbours(step, d, f, a), source, axis=1) - tr[d, f, rows, :]
                for f in range(FIELDS)
            ]
            inv, lam, mu, speed = [coef[i, rows, :] for i in range(4)]
            stiff = lam + 2.0 * mu
            if d == 0:
                lam_v = lam * w[0]
                flux = [inv * w[3], inv * w[6], inv * w[8], stiff * w[0], lam_v, lam_v,
                        mu * w[1], None, mu * w[2]]
            elif d == 1:
                lam_v = lam * w[1]
                flux = [inv * w[6], inv * w[4], inv * w[7], lam_v, stiff * w[1], lam_v,
                        mu * w[0], mu * w[2], None]
            else:
                lam_v = lam * w[2]
                flux = [inv * w[8], inv * w[7], inv * w[5], lam_v, lam_v, stiff * w[2],
                        None, mu * w[1], mu * w[0]]
            for f in range(FIELDS):
                fixed = speed * w[f]
                if flux[f] is not None:
                    fixed = fixed + sign * flux[f]
                fixed = 0.5 * fixed
                if d == 0:
                    cx[f, rows, :] = fixed
                else:
                    tr[d, f, rows, :] = fixed
        if d:
            part = slice(128 * (d - 1), 128 * d)
            for f in range(FIELDS):
                ch[rows_of(f), part], cl[rows_of(f), part] = halves(tr[d, f])

    def step_body(step, carry):
        advance(True, SERIES[1])
        advance(False, SERIES[2])
        for f in range(FIELDS):
            yh[hot_rows(f), :] = dot(hot_sel[...], xh[rows_of(f), :]).astype(BF16)
            yl[hot_rows(f), :] = dot(hot_sel[...], xl[rows_of(f), :]).astype(BF16)
            hot_sum[f] = jnp.zeros_like(hot_sum[f])

        def higher(k, c):
            weight = jnp.where(k == 0, SERIES[3], jnp.where(k == 1, SERIES[4], SERIES[5])).astype(F32)
            derive_hot()
            for j in range(4):
                part = slice(128 * j, 128 * (j + 1))
                for f, rate in enumerate(rates(part, hot_deriv, hot_rows, hot_coef)):
                    hot_sum[f, :, part] = hot_sum[f, :, part] + weight * rate
                    yh[hot_rows(f), part], yl[hot_rows(f), part] = halves(rate)
            return c

        lax.fori_loop(0, 3, higher, 0)
        def complete(f, parts):
            extra = jnp.concatenate([hot_sum[f, :, part] for part in parts], axis=1)
            h, l = halves(extra)
            extra = dot(hot_in_rows[...], h) + dot(hot_in_rows[...], l)
            ends = []
            for i, part in enumerate(parts):
                full = acc[f, :, part] + extra[:, 128 * i : 128 * (i + 1)]
                acc[f, :, part] = full
                xh[rows_of(f), part], xl[rows_of(f), part] = halves(full)
                ends.append(full)
            return ends

        for f in range(FIELDS):
            ends = complete(f, (slice(0, 128), slice(384, 512)))
            tr[0, f] = jnp.where(lane < 64, ends[0], ends[1])
        pack_pairs(lambda f: tr[0, f, 24:32, :], True, send_x.at[0])
        pack_pairs(lambda f: tr[0, f, 0:8, :], False, send_x.at[1])

        @pl.when(step == 0)
        def _():
            pl.semaphore_wait(barrier, arrivals)

        made = copies(step)

        def send(d):
            for k in (2 * d, 2 * d + 1):

                @pl.when(sending(k))
                def _(k=k):
                    made[k].start()

        send(0)
        for f in range(FIELDS):
            complete(f, (slice(128, 256), slice(256, 384)))
        faces = dot(xh[...], pick[...]) + dot(xl[...], pick[...])
        for f in range(FIELDS):
            tr[1, f] = faces[rows_of(f), 0:128]
            tr[2, f] = faces[rows_of(f), 128:256]
        for f in range(FIELDS):
            send_z[0, f] = pack_z(f, True)
            send_z[1, f] = pack_z(f, False)
        send(2)
        pack_pairs(lambda f: pack_rows_y(f, 6), True, send_y.at[0])
        pack_pairs(lambda f: pack_rows_y(f, 0), False, send_y.at[1])
        send(1)
        derive()
        for j in range(4):
            part = slice(128 * j, 128 * (j + 1))
            for f, rate in enumerate(rates(part)):
                acc[f, :, part] = q[f, :, part] + DT_STEP * rate

        def receive(d):
            for k in (2 * d, 2 * d + 1):

                @pl.when(receiving(k))
                def _(k=k):
                    made[k].wait_recv()

        receive(1)
        corrections(step, 1)
        receive(2)
        corrections(step, 2)
        spread[...] = dot(ch[...], lift[...]) + dot(cl[...], lift[...])
        for f in range(FIELDS):
            for j in range(4):
                part = slice(128 * j, 128 * (j + 1))
                full = acc[f, :, part] + (DT_STEP * LIFT_COEF) * spread[rows_of(f), part]
                if j in (1, 2):
                    q[f, :, part] = full
                    xh[rows_of(f), part], xl[rows_of(f), part] = halves(full)
                else:
                    acc[f, :, part] = full
        receive(0)
        corrections(step, 0)
        for f in range(FIELDS):
            for j, mine in ((0, lane < 64), (3, lane >= 64)):
                part = slice(128 * j, 128 * (j + 1))
                full = acc[f, :, part] + jnp.where(mine, (DT_STEP * LIFT_COEF) * cx[f], 0.0)
                q[f, :, part] = full
                xh[rows_of(f), part], xl[rows_of(f), part] = halves(full)
        for k in range(6):

            @pl.when(sending(k))
            def _(k=k):
                made[k].wait_send()

        return carry

    lax.fori_loop(0, STEPS, step_body, 0)


def shards(
    wavefield, deriv_ops, density, lame_first, shear_modulus, high_order, element_cell, face_orient
):
    wave = jnp.swapaxes(wavefield[0, 0, 0], 0, 1)
    row = (1, ELEMENTS)
    vmem = pl.BlockSpec(memory_space=pltpu.VMEM)
    any_space = pl.BlockSpec(memory_space=pltpu.HBM)
    field = (FIELDS, ELEMENTS, NODES)
    total = FIELDS * ELEMENTS
    state = pl.pallas_call(
        kernel,
        out_shape=(
            jax.ShapeDtypeStruct(field, F32),
            jax.ShapeDtypeStruct((ELEMENTS, ELEMENTS), F32),
        ),
        in_specs=[any_space] * 8,
        out_specs=(vmem, vmem),
        scratch_shapes=[
            pltpu.VMEM(field, F32),
            pltpu.VMEM(row, F32),
            pltpu.VMEM(row, F32),
            pltpu.VMEM(row, F32),
            pltpu.VMEM(row, I32),
            pltpu.VMEM(row, I32),
            pltpu.VMEM((6, 1, ELEMENTS), I32),
            pltpu.VMEM((3, NODES, NODES), F32),
            pltpu.VMEM((3, NODES, NODES), BF16),
            pltpu.VMEM((3, NODES, NODES), BF16),
            pltpu.VMEM((16, ELEMENTS), F32),
            pltpu.VMEM((4, ELEMENTS, 128), F32),
            pltpu.VMEM((3, ELEMENTS, 128), I32),
            pltpu.VMEM(field, F32),
            pltpu.VMEM((total, NODES), BF16),
            pltpu.VMEM((total, NODES), BF16),
            pltpu.VMEM((3, 6 * ELEMENTS, NODES), F32),
            pltpu.VMEM((NODES, 256), BF16),
            pltpu.VMEM((256, NODES), BF16),
            pltpu.VMEM((3, FIELDS, ELEMENTS, 128), F32),
            pltpu.VMEM((total, 256), BF16),
            pltpu.VMEM((total, 256), BF16),
            pltpu.VMEM((FIELDS, ELEMENTS, 128), F32),
            pltpu.VMEM((total, NODES), F32),
            pltpu.VMEM((ELEMENTS, HOT), BF16),
            pltpu.VMEM((3, HOT, 128), F32),
            pltpu.VMEM((FIELDS, HOT, NODES), F32),
            pltpu.VMEM((FIELDS * HOT, NODES), BF16),
            pltpu.VMEM((FIELDS * HOT, NODES), BF16),
            pltpu.VMEM((3, 6 * HOT, NODES), F32),
            pltpu.VMEM((HOT, ELEMENTS), BF16),
            pltpu.VMEM((2, 5, 8, 128), F32),
            pltpu.VMEM((2, 5, 8, 128), F32),
            pltpu.VMEM((2, FIELDS, 8, 128), F32),
            pltpu.VMEM((STEPS, 2, 5, 8, 128), F32),
            pltpu.VMEM((STEPS, 2, 5, 8, 128), F32),
            pltpu.VMEM((STEPS, 2, FIELDS, 8, 128), F32),
            pltpu.SemaphoreType.DMA((FIELDS,)),
            pltpu.SemaphoreType.DMA((3,)),
            pltpu.SemaphoreType.DMA((STEPS, 6)),
            pltpu.SemaphoreType.DMA((STEPS, 6)),
        ],
        compiler_params=pltpu.CompilerParams(
            collective_id=0, has_side_effects=True, vmem_limit_bytes=24 * 1024 * 1024
        ),
        name="elastic_steps",
    )(
        *(
            pltpu.with_memory_space_constraint(x, pltpu.HBM)
            for x in (
                wave,
                deriv_ops,
                density.reshape(row),
                lame_first.reshape(row),
                shear_modulus.reshape(row),
                high_order.reshape(row),
                element_cell.reshape(row),
                face_orient.reshape(6, 1, ELEMENTS),
            )
        ),
    )
    result = pl.pallas_call(
        restore,
        out_shape=jax.ShapeDtypeStruct(field, F32),
        in_specs=[vmem, vmem],
        out_specs=any_space,
        scratch_shapes=[pltpu.VMEM(field, F32), pltpu.SemaphoreType.DMA((FIELDS,))],
        compiler_params=pltpu.CompilerParams(vmem_limit_bytes=8 * 1024 * 1024),
        name="restore",
    )(*state)
    return jnp.swapaxes(result, 0, 1)[None, None, None]


def solution(mesh):
    row = P("gx", "gy", "ha", None)
    whole = P("gx", "gy", "ha", None, None, None)
    return jax.shard_map(
        shards,
        mesh=mesh,
        in_specs=(whole, P(), row, row, row, row, row, P("gx", "gy", "ha", None, None)),
        out_specs=whole,
        check_vma=False,
    )
```

```python
import math

import jax
import jax.numpy as jnp
from jax import lax
from jax.experimental import pallas as pl
from jax.experimental.pallas import tpu as pltpu
from jax.sharding import PartitionSpec as P

ELEMENTS = 32
HOT = 16
FIELDS = 9
NODES = 512
STEPS = 2
DT_STEP = 0.8
LIFT_COEF = 2.0
X_FIELDS = (0, 1, 2, 3, 6, 8)
Y_FIELDS = (0, 1, 2, 6, 4, 7)
Z_FIELDS = (0, 1, 2, 8, 7, 5)
AXIS_FIELDS = (X_FIELDS, Y_FIELDS, Z_FIELDS)
MESH_AXES = ("gx", "gy", "ha")
SERIES = tuple(DT_STEP**k / math.factorial(k + 1) for k in range(6))
F32 = jnp.float32
BF16 = jnp.bfloat16
I32 = jnp.int32
NT = (((1,), (1,)), ((), ()))
HIGHEST = lax.Precision.HIGHEST


def dot(a, b):
    return jnp.dot(a, b, preferred_element_type=F32)


def halves(value):
    high = value.astype(BF16)
    return high, (value - high.astype(F32)).astype(BF16)


def thirds(value):
    high = value.astype(BF16)
    rest = value - high.astype(F32)
    mid = rest.astype(BF16)
    return high, mid, (rest - mid.astype(F32)).astype(BF16)


def rows_of(field):
    return slice(ELEMENTS * field, ELEMENTS * (field + 1))


def iota(shape, dim):
    return lax.broadcasted_iota(I32, shape, dim)


def face_node(column):
    face = column // 64
    p = (column // 8) % 8
    r = column % 8
    far = 7 * (face % 2)
    return jnp.where(face < 2, p * 64 + far * 8 + r, p * 64 + r * 8 + far)


def restore(state, gather, out, full, sems):
    stores = [pltpu.make_async_copy(full.at[f], out.at[f], sems.at[f]) for f in range(FIELDS)]
    gather_out = gather[...].astype(BF16)
    for f in range(FIELDS):
        full[f] = dot(gather_out, jnp.concatenate(thirds(state[f]), axis=0))
        stores[f].start()
    for store in stores:
        store.wait()


def kernel(
    wave_in, dops, dens_in, lame_in, shear_in, hot_in, cell_in, orient_in, q, gather_out,
    wave, dens, lame, shear, hot, cell, orient,
    wf, wh, wl, small, coef, index, acc, xh, xl, deriv, pick, lift, tr, ch, cl, cx, spread,
    hot_in_rows, hot_coef, hot_sum, yh, yl, hot_deriv, hot_sel,
    send_x, send_y, send_z, recv_x, recv_y, recv_z, small_sem, load_sem, send_sem, recv_sem,
):
    barrier = pltpu.get_barrier_semaphore()
    place = [lax.axis_index(a) for a in MESH_AXES]
    count = [lax.axis_size(a) for a in MESH_AXES]
    up = [{a: lax.rem(i + 1, n)} for a, i, n in zip(MESH_AXES, place, count)]
    down = [{a: lax.rem(i + n - 1, n)} for a, i, n in zip(MESH_AXES, place, count)]
    small_loads = [
        pltpu.make_async_copy(source, dest, small_sem.at[i])
        for i, (source, dest) in enumerate(
            (
                (cell_in, cell), (hot_in, hot), (dens_in, dens), (lame_in, lame),
                (shear_in, shear), (orient_in, orient), (wave_in, wave),
            )
        )
    ]
    for load in small_loads:
        load.start()
    loads = [pltpu.make_async_copy(dops.at[a], wf.at[a], load_sem.at[a]) for a in range(3)]
    for load in loads:
        load.start()

    arrivals = 0
    for d in range(3):
        for target, steps_left in ((up[d], count[d] - 1 - place[d]), (down[d], place[d])):

            @pl.when(steps_left > 0)
            def _(target=target):
                pl.semaphore_signal(barrier, 1, device_id=target, device_id_type=pl.DeviceIdType.MESH)

            arrivals = arrivals + lax.div(steps_left + count[d] - 1, count[d])

    pick[...] = (iota((NODES, 256), 0) == face_node(iota((NODES, 256), 1))).astype(BF16)
    lift[...] = (iota((256, NODES), 1) == face_node(iota((256, NODES), 0))).astype(BF16)

    for recv, at, n in zip((recv_x, recv_y, recv_z), place, count):
        for edge, slot in ((0, 0), (n - 1, 1)):

            @pl.when(at == edge)
            def _(recv=recv, slot=slot):
                for s in range(STEPS):
                    recv[s, slot] = jnp.zeros_like(recv[s, slot])

    def derive():
        for a, fields in enumerate(AXIS_FIELDS):
            h = jnp.concatenate([xh[rows_of(f), :] for f in fields], axis=0)
            l = jnp.concatenate([xl[rows_of(f), :] for f in fields], axis=0)
            deriv[a] = dot(h, wh[a]) + dot(l, wh[a]) + dot(h, wl[a])

    small[...] = jnp.zeros_like(small)
    for load in small_loads[:-1]:
        load.wait()
    small[0:1, :] = dens[...]
    small[1:2, :] = lame[...]
    small[2:3, :] = shear[...]
    small[3:4, :] = hot[...].astype(F32)
    for i in range(6):
        small[4 + i : 5 + i, :] = orient[i].astype(F32)
    small[10:11, :] = cell[...].astype(F32)
    square = (ELEMENTS, ELEMENTS)
    place_cell = (iota(square, 0) == jnp.broadcast_to(cell[...], square)).astype(F32)
    same = (iota(square, 0) == iota(square, 1)).astype(BF16)
    cell_row = jnp.broadcast_to(cell[...], (8, ELEMENTS)).astype(F32).astype(BF16)
    cell_col = lax.dot_general(same, cell_row, NT, preferred_element_type=F32)[:, 0:1]
    triple = (ELEMENTS, 3 * ELEMENTS)
    gather_out[...] = (cell_col.astype(I32) == iota(triple, 1) % ELEMENTS).astype(F32)
    by_cell = lax.dot_general(place_cell, small[...], NT, precision=HIGHEST)
    wide = (ELEMENTS, 128)
    inv_rho = 1.0 / by_cell[:, 0:1]
    lame_col = by_cell[:, 1:2]
    shear_col = by_cell[:, 2:3]
    coef[0] = jnp.broadcast_to(inv_rho, wide)
    coef[1] = jnp.broadcast_to(lame_col, wide)
    coef[2] = jnp.broadcast_to(shear_col, wide)
    coef[3] = jnp.broadcast_to(jnp.sqrt((lame_col + 2.0 * shear_col) * inv_rho), wide)
    lane = iota(wide, 1)
    p_pos = (lane // 8) % 8
    r_pos = lane % 8
    for d in range(3):
        low = jnp.broadcast_to(by_cell[:, 4 + 2 * d : 5 + 2 * d], wide)
        high = jnp.broadcast_to(by_cell[:, 5 + 2 * d : 6 + 2 * d], wide)
        code = jnp.where(lane < 64, low, high).astype(I32)
        p_src = jnp.where((code & 1) != 0, 7 - p_pos, p_pos)
        r_src = jnp.where((code & 2) != 0, 7 - r_pos, r_pos)
        node = jnp.where((code & 4) != 0, r_src * 8 + p_src, p_src * 8 + r_src)
        index[d] = node + jnp.where(lane < 64, 64, 0)
    slots = (HOT, ELEMENTS)
    flag_row = lax.dot_general(small[...], place_cell, NT, precision=HIGHEST)[3:4, :]
    upto = (iota(square, 0) <= iota(square, 1)).astype(F32)
    rank_row = lax.dot_general(
        jnp.broadcast_to(flag_row, (8, ELEMENTS)), upto, (((1,), (0,)), ((), ())), precision=HIGHEST
    )[0:1, :].astype(I32)
    chosen = (iota(slots, 0) + 1 == jnp.broadcast_to(rank_row, slots)) & (
        jnp.broadcast_to(flag_row, slots) > 0.5
    )
    select = chosen.astype(F32)
    hot_sel[...] = select.astype(BF16)
    of_slot = lax.dot_general(select, by_cell, (((1,), (0,)), ((), ())), precision=HIGHEST)
    filled = of_slot[:, 0:1] > 0.0
    hot_coef[0] = jnp.broadcast_to(
        jnp.where(filled, 1.0 / jnp.where(filled, of_slot[:, 0:1], 1.0), 0.0), (HOT, 128)
    )
    hot_coef[1] = jnp.broadcast_to(of_slot[:, 1:2], (HOT, 128))
    hot_coef[2] = jnp.broadcast_to(of_slot[:, 2:3], (HOT, 128))
    slot_col = iota((ELEMENTS, 2 * HOT), 1) % HOT + 1
    below = (iota(square, 1) <= iota(square, 0)).astype(F32)
    rank_col = lax.dot_general(
        below, jnp.broadcast_to(by_cell[:, 3:4], (ELEMENTS, 8)), (((1,), (0,)), ((), ())), precision=HIGHEST
    )[:, 0:1]
    back = (slot_col == rank_col.astype(I32)) & (by_cell[:, 3:4] > 0.5)
    hot_in_rows[...] = back.astype(BF16)
    gather_in = place_cell.astype(BF16)
    small_loads[-1].wait()
    for f in range(FIELDS):
        a, b, c = thirds(wave[f])
        full = dot(gather_in, a) + dot(gather_in, b) + dot(gather_in, c)
        q[f] = full
        xh[rows_of(f), :], xl[rows_of(f), :] = halves(full)

    for a in range(3):
        loads[a].wait()

        def split(i, carry, a=a):
            part = pl.ds(pl.multiple_of(i * 64, 64), 64)
            h, l = halves(wf[a, part, :])
            wh[a, part, :] = h
            wl[a, part, :] = l
            return carry

        lax.fori_loop(0, NODES // 64, split, 0)

    def hot_rows(field):
        return slice(HOT * field, HOT * (field + 1))

    def derive_hot():
        for a, fields in enumerate(AXIS_FIELDS):
            h = [yh[hot_rows(f), :] for f in fields]
            l = [yl[hot_rows(f), :] for f in fields]
            both = dot(jnp.concatenate(h + l, axis=0), wh[a])
            cross = dot(jnp.concatenate(h, axis=0), wl[a])
            hot_deriv[a] = both[0 : 6 * HOT] + (both[6 * HOT :] + cross)

    def rates(part, source=deriv, rows=rows_of, factors=coef):
        x = [source[0, rows(i), part] for i in range(6)]
        y = [source[1, rows(i), part] for i in range(6)]
        z = [source[2, rows(i), part] for i in range(6)]
        inv, lam, mu = factors[0], factors[1], factors[2]
        lam_div = lam * (x[0] + y[1] + z[2])
        mu2 = 2.0 * mu
        return [
            inv * (x[3] + y[3] + z[3]),
            inv * (x[4] + y[4] + z[4]),
            inv * (x[5] + y[5] + z[5]),
            lam_div + mu2 * x[0],
            lam_div + mu2 * y[1],
            lam_div + mu2 * z[2],
            mu * (x[1] + y[0]),
            mu * (y[2] + z[1]),
            mu * (x[2] + z[0]),
        ]

    def advance(first, weight):
        derive()
        for j in range(4):
            part = slice(128 * j, 128 * (j + 1))
            for f, rate in enumerate(rates(part)):
                term = weight * rate
                base = q if first else acc
                acc[f, :, part] = base[f, :, part] + term
                xh[rows_of(f), part], xl[rows_of(f), part] = halves(rate)

    def pack_pairs(tile, upper, dest):
        keep = (iota((8, 128), 1) >= 64) if upper else (iota((8, 128), 1) < 64)
        for f in range(4):
            dest[f] = jnp.where(keep, tile(f), pltpu.roll(tile(f + 5), 64, 1))
        dest[4] = tile(4)

    def unpack_pairs(source, f):
        return source[f] if f < 5 else pltpu.roll(source[f - 5], 64, 1)

    sub = iota((8, 128), 0)
    lo_lane = iota((8, 128), 1) < 64
    even = sub % 2 == 0

    def pack_rows_y(f, first_row):
        result = None
        for a in range(4):
            tile = tr[1, f, 8 * a : 8 * a + 8, :]
            shift = (2 * a - first_row) % 8
            moved = pltpu.roll(tile, shift, 0) if shift else tile
            result = moved if a == 0 else jnp.where(sub // 2 == a, moved, result)
        return result

    def pack_z(f, odd):
        strips = []
        for a in range(2):
            one = tr[2, f, 8 * a : 8 * a + 8, :]
            two = tr[2, f, 8 * a + 16 : 8 * a + 24, :]
            if odd:
                strips.append(jnp.where(even, pltpu.roll(two, 7, 0), one))
            else:
                strips.append(jnp.where(even, one, pltpu.roll(two, 1, 0)))
        keep = jnp.logical_not(lo_lane) if odd else lo_lane
        return jnp.where(keep, strips[0], pltpu.roll(strips[1], 64, 1))

    sends = (send_x, send_y, send_z)
    recvs = (recv_x, recv_y, recv_z)

    def copies(step):
        made = []
        for d in range(3):
            for way, target in ((0, up[d]), (1, down[d])):
                made.append(
                    pltpu.make_async_remote_copy(
                        src_ref=sends[d].at[way],
                        dst_ref=recvs[d].at[step, way],
                        send_sem=send_sem.at[step, 2 * d + way],
                        recv_sem=recv_sem.at[step, 2 * d + way],
                        device_id=target,
                        device_id_type=pl.DeviceIdType.MESH,
                    )
                )
        return made

    def sending(k):
        d, way = divmod(k, 2)
        return place[d] < count[d] - 1 if way == 0 else place[d] > 0

    def receiving(k):
        d, way = divmod(k, 2)
        return place[d] > 0 if way == 0 else place[d] < count[d] - 1

    def neighbours(step, d, f, a):
        tile = tr[d, f, 8 * a : 8 * a + 8, :]
        if d == 0:
            before = unpack_pairs(recv_x.at[step, 0], f) if a == 0 else tr[0, f, 8 * a - 8 : 8 * a, :]
            after = unpack_pairs(recv_x.at[step, 1], f) if a == 3 else tr[0, f, 8 * a + 8 : 8 * a + 16, :]
        elif d == 1:
            low = unpack_pairs(recv_y.at[step, 0], f)
            low = pltpu.roll(low, (8 - 2 * a) % 8, 0) if a else low
            before = jnp.where(sub < 2, low, pltpu.roll(tile, 2, 0))
            high = unpack_pairs(recv_y.at[step, 1], f)
            high = pltpu.roll(high, (6 - 2 * a) % 8, 0) if a < 3 else high
            after = jnp.where(sub >= 6, high, pltpu.roll(tile, 6, 0))
        else:
            low = recv_z[step, 0, f]
            high = recv_z[step, 1, f]
            if a % 2:
                low = pltpu.roll(low, 64, 1)
                high = pltpu.roll(high, 64, 1)
            if a < 2:
                low = pltpu.roll(low, 7, 0)
                high = pltpu.roll(high, 1, 0)
            before = jnp.where(even, low, pltpu.roll(tile, 1, 0))
            after = jnp.where(even, pltpu.roll(tile, 7, 0), high)
        return jnp.where(lo_lane, after, before)

    def corrections(step, d):
        sign = jnp.where(lo_lane, -1.0, 1.0)
        for a in range(4):
            rows = slice(8 * a, 8 * a + 8)
            source = index[d, rows, :]
            w = [
                jnp.take_along_axis(neighbours(step, d, f, a), source, axis=1) - tr[d, f, rows, :]
                for f in range(FIELDS)
            ]
            inv, lam, mu, speed = [coef[i, rows, :] for i in range(4)]
            stiff = lam + 2.0 * mu
            if d == 0:
                lam_v = lam * w[0]
                flux = [inv * w[3], inv * w[6], inv * w[8], stiff * w[0], lam_v, lam_v,
                        mu * w[1], None, mu * w[2]]
            elif d == 1:
                lam_v = lam * w[1]
                flux = [inv * w[6], inv * w[4], inv * w[7], lam_v, stiff * w[1], lam_v,
                        mu * w[0], mu * w[2], None]
            else:
                lam_v = lam * w[2]
                flux = [inv * w[8], inv * w[7], inv * w[5], lam_v, lam_v, stiff * w[2],
                        None, mu * w[1], mu * w[0]]
            for f in range(FIELDS):
                fixed = speed * w[f]
                if flux[f] is not None:
                    fixed = fixed + sign * flux[f]
                fixed = 0.5 * fixed
                if d == 0:
                    cx[f, rows, :] = fixed
                else:
                    tr[d, f, rows, :] = fixed
        if d:
            part = slice(128 * (d - 1), 128 * d)
            for f in range(FIELDS):
                ch[rows_of(f), part], cl[rows_of(f), part] = halves(tr[d, f])

    def step_body(step, carry):
        advance(True, SERIES[1])
        advance(False, SERIES[2])
        for f in range(FIELDS):
            yh[hot_rows(f), :] = dot(hot_sel[...], xh[rows_of(f), :]).astype(BF16)
            yl[hot_rows(f), :] = dot(hot_sel[...], xl[rows_of(f), :]).astype(BF16)
            hot_sum[f] = jnp.zeros_like(hot_sum[f])

        def higher(k, c):
            weight = jnp.where(k == 0, SERIES[3], jnp.where(k == 1, SERIES[4], SERIES[5])).astype(F32)
            derive_hot()
            for j in range(4):
                part = slice(128 * j, 128 * (j + 1))
                for f, rate in enumerate(rates(part, hot_deriv, hot_rows, hot_coef)):
                    hot_sum[f, :, part] = hot_sum[f, :, part] + weight * rate
                    yh[hot_rows(f), part], yl[hot_rows(f), part] = halves(rate)
            return c

        lax.fori_loop(0, 3, higher, 0)
        def complete(f, parts):
            extra = jnp.concatenate([hot_sum[f, :, part] for part in parts], axis=1)
            extra = dot(hot_in_rows[...], jnp.concatenate(halves(extra), axis=0))
            ends = []
            for i, part in enumerate(parts):
                full = acc[f, :, part] + extra[:, 128 * i : 128 * (i + 1)]
                acc[f, :, part] = full
                xh[rows_of(f), part], xl[rows_of(f), part] = halves(full)
                ends.append(full)
            return ends

        for f in range(FIELDS):
            ends = complete(f, (slice(0, 128), slice(384, 512)))
            tr[0, f] = jnp.where(lane < 64, ends[0], ends[1])
        pack_pairs(lambda f: tr[0, f, 24:32, :], True, send_x.at[0])
        pack_pairs(lambda f: tr[0, f, 0:8, :], False, send_x.at[1])

        @pl.when(step == 0)
        def _():
            pl.semaphore_wait(barrier, arrivals)

        made = copies(step)

        def send(d):
            for k in (2 * d, 2 * d + 1):

                @pl.when(sending(k))
                def _(k=k):
                    made[k].start()

        send(0)
        for f in range(FIELDS):
            complete(f, (slice(128, 256), slice(256, 384)))
        faces = dot(xh[...], pick[...]) + dot(xl[...], pick[...])
        for f in range(FIELDS):
            tr[1, f] = faces[rows_of(f), 0:128]
            tr[2, f] = faces[rows_of(f), 128:256]
        for f in range(FIELDS):
            send_z[0, f] = pack_z(f, True)
            send_z[1, f] = pack_z(f, False)
        send(2)
        pack_pairs(lambda f: pack_rows_y(f, 6), True, send_y.at[0])
        pack_pairs(lambda f: pack_rows_y(f, 0), False, send_y.at[1])
        send(1)
        derive()
        for j in range(4):
            part = slice(128 * j, 128 * (j + 1))
            for f, rate in enumerate(rates(part)):
                acc[f, :, part] = q[f, :, part] + DT_STEP * rate

        def receive(d):
            for k in (2 * d, 2 * d + 1):

                @pl.when(receiving(k))
                def _(k=k):
                    made[k].wait_recv()

        receive(1)
        corrections(step, 1)
        receive(2)
        corrections(step, 2)
        spread[...] = dot(ch[...], lift[...]) + dot(cl[...], lift[...])
        for f in range(FIELDS):
            for j in range(4):
                part = slice(128 * j, 128 * (j + 1))
                full = acc[f, :, part] + (DT_STEP * LIFT_COEF) * spread[rows_of(f), part]
                if j in (1, 2):
                    q[f, :, part] = full
                    xh[rows_of(f), part], xl[rows_of(f), part] = halves(full)
                else:
                    acc[f, :, part] = full
        receive(0)
        corrections(step, 0)
        for f in range(FIELDS):
            for j, mine in ((0, lane < 64), (3, lane >= 64)):
                part = slice(128 * j, 128 * (j + 1))
                full = acc[f, :, part] + jnp.where(mine, (DT_STEP * LIFT_COEF) * cx[f], 0.0)
                q[f, :, part] = full
                xh[rows_of(f), part], xl[rows_of(f), part] = halves(full)
        for k in range(6):

            @pl.when(sending(k))
            def _(k=k):
                made[k].wait_send()

        return carry

    lax.fori_loop(0, STEPS, step_body, 0)


def shards(
    wavefield, deriv_ops, density, lame_first, shear_modulus, high_order, element_cell, face_orient
):
    wave = jnp.swapaxes(wavefield[0, 0, 0], 0, 1)
    row = (1, ELEMENTS)
    vmem = pl.BlockSpec(memory_space=pltpu.VMEM)
    any_space = pl.BlockSpec(memory_space=pltpu.HBM)
    field = (FIELDS, ELEMENTS, NODES)
    total = FIELDS * ELEMENTS
    state = pl.pallas_call(
        kernel,
        out_shape=(
            jax.ShapeDtypeStruct(field, F32),
            jax.ShapeDtypeStruct((ELEMENTS, 3 * ELEMENTS), F32),
        ),
        in_specs=[any_space] * 8,
        out_specs=(vmem, vmem),
        scratch_shapes=[
            pltpu.VMEM(field, F32),
            pltpu.VMEM(row, F32),
            pltpu.VMEM(row, F32),
            pltpu.VMEM(row, F32),
            pltpu.VMEM(row, I32),
            pltpu.VMEM(row, I32),
            pltpu.VMEM((6, 1, ELEMENTS), I32),
            pltpu.VMEM((3, NODES, NODES), F32),
            pltpu.VMEM((3, NODES, NODES), BF16),
            pltpu.VMEM((3, NODES, NODES), BF16),
            pltpu.VMEM((16, ELEMENTS), F32),
            pltpu.VMEM((4, ELEMENTS, 128), F32),
            pltpu.VMEM((3, ELEMENTS, 128), I32),
            pltpu.VMEM(field, F32),
            pltpu.VMEM((total, NODES), BF16),
            pltpu.VMEM((total, NODES), BF16),
            pltpu.VMEM((3, 6 * ELEMENTS, NODES), F32),
            pltpu.VMEM((NODES, 256), BF16),
            pltpu.VMEM((256, NODES), BF16),
            pltpu.VMEM((3, FIELDS, ELEMENTS, 128), F32),
            pltpu.VMEM((total, 256), BF16),
            pltpu.VMEM((total, 256), BF16),
            pltpu.VMEM((FIELDS, ELEMENTS, 128), F32),
            pltpu.VMEM((total, NODES), F32),
            pltpu.VMEM((ELEMENTS, 2 * HOT), BF16),
            pltpu.VMEM((3, HOT, 128), F32),
            pltpu.VMEM((FIELDS, HOT, NODES), F32),
            pltpu.VMEM((FIELDS * HOT, NODES), BF16),
            pltpu.VMEM((FIELDS * HOT, NODES), BF16),
            pltpu.VMEM((3, 6 * HOT, NODES), F32),
            pltpu.VMEM((HOT, ELEMENTS), BF16),
            pltpu.VMEM((2, 5, 8, 128), F32),
            pltpu.VMEM((2, 5, 8, 128), F32),
            pltpu.VMEM((2, FIELDS, 8, 128), F32),
            pltpu.VMEM((STEPS, 2, 5, 8, 128), F32),
            pltpu.VMEM((STEPS, 2, 5, 8, 128), F32),
            pltpu.VMEM((STEPS, 2, FIELDS, 8, 128), F32),
            pltpu.SemaphoreType.DMA((FIELDS,)),
            pltpu.SemaphoreType.DMA((3,)),
            pltpu.SemaphoreType.DMA((STEPS, 6)),
            pltpu.SemaphoreType.DMA((STEPS, 6)),
        ],
        compiler_params=pltpu.CompilerParams(
            collective_id=0, has_side_effects=True, vmem_limit_bytes=24 * 1024 * 1024
        ),
        name="elastic_steps",
    )(
        *(
            pltpu.with_memory_space_constraint(x, pltpu.HBM)
            for x in (
                wave,
                deriv_ops,
                density.reshape(row),
                lame_first.reshape(row),
                shear_modulus.reshape(row),
                high_order.reshape(row),
                element_cell.reshape(row),
                face_orient.reshape(6, 1, ELEMENTS),
            )
        ),
    )
    result = pl.pallas_call(
        restore,
        out_shape=jax.ShapeDtypeStruct(field, F32),
        in_specs=[vmem, vmem],
        out_specs=any_space,
        scratch_shapes=[pltpu.VMEM(field, F32), pltpu.SemaphoreType.DMA((FIELDS,))],
        compiler_params=pltpu.CompilerParams(vmem_limit_bytes=8 * 1024 * 1024),
        name="restore",
    )(*state)
    return jnp.swapaxes(result, 0, 1)[None, None, None]


def solution(mesh):
    row = P("gx", "gy", "ha", None)
    whole = P("gx", "gy", "ha", None, None, None)
    return jax.shard_map(
        shards,
        mesh=mesh,
        in_specs=(whole, P(), row, row, row, row, row, P("gx", "gy", "ha", None, None)),
        out_specs=whole,
        check_vma=False,
    )
```

```python
import math

import jax
import jax.numpy as jnp
from jax import lax
from jax.experimental import pallas as pl
from jax.experimental.pallas import tpu as pltpu
from jax.sharding import PartitionSpec as P

ELEMENTS = 32
HOT = 16
FIELDS = 9
NODES = 512
STEPS = 2
DT_STEP = 0.8
LIFT_COEF = 2.0
X_FIELDS = (0, 1, 2, 3, 6, 8)
Y_FIELDS = (0, 1, 2, 6, 4, 7)
Z_FIELDS = (0, 1, 2, 8, 7, 5)
AXIS_FIELDS = (X_FIELDS, Y_FIELDS, Z_FIELDS)
MESH_AXES = ("gx", "gy", "ha")
SERIES = tuple(DT_STEP**k / math.factorial(k + 1) for k in range(6))
F32 = jnp.float32
BF16 = jnp.bfloat16
I32 = jnp.int32
NT = (((1,), (1,)), ((), ()))
HIGHEST = lax.Precision.HIGHEST


def dot(a, b):
    return jnp.dot(a, b, preferred_element_type=F32)


def halves(value):
    high = value.astype(BF16)
    return high, (value - high.astype(F32)).astype(BF16)


def thirds(value):
    high = value.astype(BF16)
    rest = value - high.astype(F32)
    mid = rest.astype(BF16)
    return high, mid, (rest - mid.astype(F32)).astype(BF16)


def rows_of(field):
    return slice(ELEMENTS * field, ELEMENTS * (field + 1))


def iota(shape, dim):
    return lax.broadcasted_iota(I32, shape, dim)


def face_node(column):
    face = column // 64
    p = (column // 8) % 8
    r = column % 8
    far = 7 * (face % 2)
    return jnp.where(face < 2, p * 64 + far * 8 + r, p * 64 + r * 8 + far)


def restore(state, gather, out, full, sems):
    stores = [pltpu.make_async_copy(full.at[f], out.at[f], sems.at[f]) for f in range(FIELDS)]
    gather_out = gather[...].astype(BF16)
    for f in range(FIELDS):
        full[f] = dot(gather_out, jnp.concatenate(thirds(state[f]), axis=0))
        stores[f].start()
    for store in stores:
        store.wait()


def kernel(
    wave_in, dops, dens_in, lame_in, shear_in, hot_in, cell_in, orient_in, q, gather_out,
    wave, dens, lame, shear, hot, cell, orient,
    wf, wh, wl, small, coef, index, acc, xh, xl, deriv, pick, lift, tr, ch, cl, cx, spread,
    hot_in_rows, hot_coef, hot_sum, yh, yl, hot_deriv, hot_sel,
    send_x, send_y, send_z, recv_x, recv_y, recv_z, small_sem, load_sem, send_sem, recv_sem,
):
    barrier = pltpu.get_barrier_semaphore()
    place = [lax.axis_index(a) for a in MESH_AXES]
    count = [lax.axis_size(a) for a in MESH_AXES]
    up = [{a: lax.rem(i + 1, n)} for a, i, n in zip(MESH_AXES, place, count)]
    down = [{a: lax.rem(i + n - 1, n)} for a, i, n in zip(MESH_AXES, place, count)]
    small_loads = [
        pltpu.make_async_copy(source, dest, small_sem.at[i])
        for i, (source, dest) in enumerate(
            (
                (cell_in, cell), (hot_in, hot), (dens_in, dens), (lame_in, lame),
                (shear_in, shear), (orient_in, orient), (wave_in, wave),
            )
        )
    ]
    for load in small_loads:
        load.start()
    loads = [pltpu.make_async_copy(dops.at[a], wf.at[a], load_sem.at[a]) for a in range(3)]
    for load in loads:
        load.start()

    arrivals = 0
    for d in range(3):
        for target, steps_left in ((up[d], count[d] - 1 - place[d]), (down[d], place[d])):

            @pl.when(steps_left > 0)
            def _(target=target):
                pl.semaphore_signal(barrier, 1, device_id=target, device_id_type=pl.DeviceIdType.MESH)

            arrivals = arrivals + lax.div(steps_left + count[d] - 1, count[d])

    pick[...] = (iota((NODES, 256), 0) == face_node(iota((NODES, 256), 1))).astype(BF16)
    lift[...] = (iota((256, NODES), 1) == face_node(iota((256, NODES), 0))).astype(BF16)

    for recv, at, n in zip((recv_x, recv_y, recv_z), place, count):
        for edge, slot in ((0, 0), (n - 1, 1)):

            @pl.when(at == edge)
            def _(recv=recv, slot=slot):
                for s in range(STEPS):
                    recv[s, slot] = jnp.zeros_like(recv[s, slot])

    def derive():
        for a, fields in enumerate(AXIS_FIELDS):
            h = jnp.concatenate([xh[rows_of(f), :] for f in fields], axis=0)
            l = jnp.concatenate([xl[rows_of(f), :] for f in fields], axis=0)
            deriv[a] = dot(h, wh[a]) + dot(l, wh[a]) + dot(h, wl[a])

    small[...] = jnp.zeros_like(small)
    for load in small_loads[:-1]:
        load.wait()
    small[0:1, :] = dens[...]
    small[1:2, :] = lame[...]
    small[2:3, :] = shear[...]
    small[3:4, :] = hot[...].astype(F32)
    for i in range(6):
        small[4 + i : 5 + i, :] = orient[i].astype(F32)
    small[10:11, :] = cell[...].astype(F32)
    square = (ELEMENTS, ELEMENTS)
    place_cell = (iota(square, 0) == jnp.broadcast_to(cell[...], square)).astype(F32)
    same = (iota(square, 0) == iota(square, 1)).astype(BF16)
    cell_row = jnp.broadcast_to(cell[...], (8, ELEMENTS)).astype(F32).astype(BF16)
    cell_col = lax.dot_general(same, cell_row, NT, preferred_element_type=F32)[:, 0:1]
    triple = (ELEMENTS, 3 * ELEMENTS)
    gather_out[...] = (cell_col.astype(I32) == iota(triple, 1) % ELEMENTS).astype(F32)
    by_cell = lax.dot_general(place_cell, small[...], NT, precision=HIGHEST)
    wide = (ELEMENTS, 128)
    inv_rho = 1.0 / by_cell[:, 0:1]
    lame_col = by_cell[:, 1:2]
    shear_col = by_cell[:, 2:3]
    coef[0] = jnp.broadcast_to(inv_rho, wide)
    coef[1] = jnp.broadcast_to(lame_col, wide)
    coef[2] = jnp.broadcast_to(shear_col, wide)
    coef[3] = jnp.broadcast_to(jnp.sqrt((lame_col + 2.0 * shear_col) * inv_rho), wide)
    lane = iota(wide, 1)
    p_pos = (lane // 8) % 8
    r_pos = lane % 8
    for d in range(3):
        low = jnp.broadcast_to(by_cell[:, 4 + 2 * d : 5 + 2 * d], wide)
        high = jnp.broadcast_to(by_cell[:, 5 + 2 * d : 6 + 2 * d], wide)
        code = jnp.where(lane < 64, low, high).astype(I32)
        p_src = jnp.where((code & 1) != 0, 7 - p_pos, p_pos)
        r_src = jnp.where((code & 2) != 0, 7 - r_pos, r_pos)
        node = jnp.where((code & 4) != 0, r_src * 8 + p_src, p_src * 8 + r_src)
        index[d] = node + jnp.where(lane < 64, 64, 0)
    slots = (HOT, ELEMENTS)
    flag_row = lax.dot_general(small[...], place_cell, NT, precision=HIGHEST)[3:4, :]
    upto = (iota(square, 0) <= iota(square, 1)).astype(F32)
    rank_row = lax.dot_general(
        jnp.broadcast_to(flag_row, (8, ELEMENTS)), upto, (((1,), (0,)), ((), ())), precision=HIGHEST
    )[0:1, :].astype(I32)
    chosen = (iota(slots, 0) + 1 == jnp.broadcast_to(rank_row, slots)) & (
        jnp.broadcast_to(flag_row, slots) > 0.5
    )
    select = chosen.astype(F32)
    hot_sel[...] = select.astype(BF16)
    of_slot = lax.dot_general(select, by_cell, (((1,), (0,)), ((), ())), precision=HIGHEST)
    filled = of_slot[:, 0:1] > 0.0
    hot_coef[0] = jnp.broadcast_to(
        jnp.where(filled, 1.0 / jnp.where(filled, of_slot[:, 0:1], 1.0), 0.0), (HOT, 128)
    )
    hot_coef[1] = jnp.broadcast_to(of_slot[:, 1:2], (HOT, 128))
    hot_coef[2] = jnp.broadcast_to(of_slot[:, 2:3], (HOT, 128))
    slot_col = iota((ELEMENTS, 2 * HOT), 1) % HOT + 1
    below = (iota(square, 1) <= iota(square, 0)).astype(F32)
    rank_col = lax.dot_general(
        below, jnp.broadcast_to(by_cell[:, 3:4], (ELEMENTS, 8)), (((1,), (0,)), ((), ())), precision=HIGHEST
    )[:, 0:1]
    back = (slot_col == rank_col.astype(I32)) & (by_cell[:, 3:4] > 0.5)
    hot_in_rows[...] = back.astype(BF16)
    cells = jnp.concatenate([cell[...]] * 3, axis=1)
    gather_in = (iota(triple, 0) == jnp.broadcast_to(cells, triple)).astype(BF16)
    small_loads[-1].wait()
    for f in range(FIELDS):
        full = dot(gather_in, jnp.concatenate(thirds(wave[f]), axis=0))
        q[f] = full
        xh[rows_of(f), :], xl[rows_of(f), :] = halves(full)

    for a in range(3):
        loads[a].wait()

        def split(i, carry, a=a):
            part = pl.ds(pl.multiple_of(i * 64, 64), 64)
            h, l = halves(wf[a, part, :])
            wh[a, part, :] = h
            wl[a, part, :] = l
            return carry

        lax.fori_loop(0, NODES // 64, split, 0)

    def hot_rows(field):
        return slice(HOT * field, HOT * (field + 1))

    def derive_hot(parts=(slice(0, NODES),)):
        for a, fields in enumerate(AXIS_FIELDS):
            h = [yh[hot_rows(f), :] for f in fields]
            l = [yl[hot_rows(f), :] for f in fields]
            right = jnp.concatenate([wh[a, :, part] for part in parts], axis=1)
            both = dot(jnp.concatenate(h + l, axis=0), right)
            right = jnp.concatenate([wl[a, :, part] for part in parts], axis=1)
            cross = dot(jnp.concatenate(h, axis=0), right)
            total = both[0 : 6 * HOT] + (both[6 * HOT :] + cross)
            at = 0
            for part in parts:
                width = part.stop - part.start
                hot_deriv[a, :, part] = total[:, at : at + width]
                at += width

    def rates(part, source=deriv, rows=rows_of, factors=coef):
        x = [source[0, rows(i), part] for i in range(6)]
        y = [source[1, rows(i), part] for i in range(6)]
        z = [source[2, rows(i), part] for i in range(6)]
        inv, lam, mu = factors[0], factors[1], factors[2]
        lam_div = lam * (x[0] + y[1] + z[2])
        mu2 = 2.0 * mu
        return [
            inv * (x[3] + y[3] + z[3]),
            inv * (x[4] + y[4] + z[4]),
            inv * (x[5] + y[5] + z[5]),
            lam_div + mu2 * x[0],
            lam_div + mu2 * y[1],
            lam_div + mu2 * z[2],
            mu * (x[1] + y[0]),
            mu * (y[2] + z[1]),
            mu * (x[2] + z[0]),
        ]

    def advance(first, weight):
        derive()
        for j in range(4):
            part = slice(128 * j, 128 * (j + 1))
            for f, rate in enumerate(rates(part)):
                term = weight * rate
                base = q if first else acc
                acc[f, :, part] = base[f, :, part] + term
                xh[rows_of(f), part], xl[rows_of(f), part] = halves(rate)

    def pack_pairs(tile, upper, dest):
        keep = (iota((8, 128), 1) >= 64) if upper else (iota((8, 128), 1) < 64)
        for f in range(4):
            dest[f] = jnp.where(keep, tile(f), pltpu.roll(tile(f + 5), 64, 1))
        dest[4] = tile(4)

    def unpack_pairs(source, f):
        return source[f] if f < 5 else pltpu.roll(source[f - 5], 64, 1)

    sub = iota((8, 128), 0)
    lo_lane = iota((8, 128), 1) < 64
    even = sub % 2 == 0

    def pack_rows_y(f, first_row):
        result = None
        for a in range(4):
            tile = tr[1, f, 8 * a : 8 * a + 8, :]
            shift = (2 * a - first_row) % 8
            moved = pltpu.roll(tile, shift, 0) if shift else tile
            result = moved if a == 0 else jnp.where(sub // 2 == a, moved, result)
        return result

    def pack_z(f, odd):
        strips = []
        for a in range(2):
            one = tr[2, f, 8 * a : 8 * a + 8, :]
            two = tr[2, f, 8 * a + 16 : 8 * a + 24, :]
            if odd:
                strips.append(jnp.where(even, pltpu.roll(two, 7, 0), one))
            else:
                strips.append(jnp.where(even, one, pltpu.roll(two, 1, 0)))
        keep = jnp.logical_not(lo_lane) if odd else lo_lane
        return jnp.where(keep, strips[0], pltpu.roll(strips[1], 64, 1))

    sends = (send_x, send_y, send_z)
    recvs = (recv_x, recv_y, recv_z)

    def copies(step):
        made = []
        for d in range(3):
            for way, target in ((0, up[d]), (1, down[d])):
                made.append(
                    pltpu.make_async_remote_copy(
                        src_ref=sends[d].at[way],
                        dst_ref=recvs[d].at[step, way],
                        send_sem=send_sem.at[step, 2 * d + way],
                        recv_sem=recv_sem.at[step, 2 * d + way],
                        device_id=target,
                        device_id_type=pl.DeviceIdType.MESH,
                    )
                )
        return made

    def sending(k):
        d, way = divmod(k, 2)
        return place[d] < count[d] - 1 if way == 0 else place[d] > 0

    def receiving(k):
        d, way = divmod(k, 2)
        return place[d] > 0 if way == 0 else place[d] < count[d] - 1

    def neighbours(step, d, f, a):
        tile = tr[d, f, 8 * a : 8 * a + 8, :]
        if d == 0:
            before = unpack_pairs(recv_x.at[step, 0], f) if a == 0 else tr[0, f, 8 * a - 8 : 8 * a, :]
            after = unpack_pairs(recv_x.at[step, 1], f) if a == 3 else tr[0, f, 8 * a + 8 : 8 * a + 16, :]
        elif d == 1:
            low = unpack_pairs(recv_y.at[step, 0], f)
            low = pltpu.roll(low, (8 - 2 * a) % 8, 0) if a else low
            before = jnp.where(sub < 2, low, pltpu.roll(tile, 2, 0))
            high = unpack_pairs(recv_y.at[step, 1], f)
            high = pltpu.roll(high, (6 - 2 * a) % 8, 0) if a < 3 else high
            after = jnp.where(sub >= 6, high, pltpu.roll(tile, 6, 0))
        else:
            low = recv_z[step, 0, f]
            high = recv_z[step, 1, f]
            if a % 2:
                low = pltpu.roll(low, 64, 1)
                high = pltpu.roll(high, 64, 1)
            if a < 2:
                low = pltpu.roll(low, 7, 0)
                high = pltpu.roll(high, 1, 0)
            before = jnp.where(even, low, pltpu.roll(tile, 1, 0))
            after = jnp.where(even, pltpu.roll(tile, 7, 0), high)
        return jnp.where(lo_lane, after, before)

    def corrections(step, d):
        sign = jnp.where(lo_lane, -1.0, 1.0)
        for a in range(4):
            rows = slice(8 * a, 8 * a + 8)
            source = index[d, rows, :]
            w = [
                jnp.take_along_axis(neighbours(step, d, f, a), source, axis=1) - tr[d, f, rows, :]
                for f in range(FIELDS)
            ]
            inv, lam, mu, speed = [coef[i, rows, :] for i in range(4)]
            stiff = lam + 2.0 * mu
            if d == 0:
                lam_v = lam * w[0]
                flux = [inv * w[3], inv * w[6], inv * w[8], stiff * w[0], lam_v, lam_v,
                        mu * w[1], None, mu * w[2]]
            elif d == 1:
                lam_v = lam * w[1]
                flux = [inv * w[6], inv * w[4], inv * w[7], lam_v, stiff * w[1], lam_v,
                        mu * w[0], mu * w[2], None]
            else:
                lam_v = lam * w[2]
                flux = [inv * w[8], inv * w[7], inv * w[5], lam_v, lam_v, stiff * w[2],
                        None, mu * w[1], mu * w[0]]
            for f in range(FIELDS):
                fixed = speed * w[f]
                if flux[f] is not None:
                    fixed = fixed + sign * flux[f]
                fixed = 0.5 * fixed
                if d == 0:
                    cx[f, rows, :] = fixed
                else:
                    tr[d, f, rows, :] = fixed
        if d:
            part = slice(128 * (d - 1), 128 * d)
            for f in range(FIELDS):
                ch[rows_of(f), part], cl[rows_of(f), part] = halves(tr[d, f])

    def step_body(step, carry):
        advance(True, SERIES[1])
        advance(False, SERIES[2])
        for f in range(FIELDS):
            yh[hot_rows(f), :] = dot(hot_sel[...], xh[rows_of(f), :]).astype(BF16)
            yl[hot_rows(f), :] = dot(hot_sel[...], xl[rows_of(f), :]).astype(BF16)
            hot_sum[f] = jnp.zeros_like(hot_sum[f])

        def higher(k, c):
            weight = jnp.where(k == 0, SERIES[3], SERIES[4]).astype(F32)
            derive_hot()
            for j in range(4):
                part = slice(128 * j, 128 * (j + 1))
                for f, rate in enumerate(rates(part, hot_deriv, hot_rows, hot_coef)):
                    hot_sum[f, :, part] = hot_sum[f, :, part] + weight * rate
                    yh[hot_rows(f), part], yl[hot_rows(f), part] = halves(rate)
            return c

        lax.fori_loop(0, 2, higher, 0)

        def last_order(parts):
            derive_hot(parts)
            for part in parts:
                for f, rate in enumerate(rates(part, hot_deriv, hot_rows, hot_coef)):
                    hot_sum[f, :, part] = hot_sum[f, :, part] + SERIES[5] * rate

        outer = (slice(0, 128), slice(384, 512))
        inner = (slice(128, 256), slice(256, 384))
        last_order(outer)
        def complete(f, parts):
            extra = jnp.concatenate([hot_sum[f, :, part] for part in parts], axis=1)
            extra = dot(hot_in_rows[...], jnp.concatenate(halves(extra), axis=0))
            ends = []
            for i, part in enumerate(parts):
                full = acc[f, :, part] + extra[:, 128 * i : 128 * (i + 1)]
                acc[f, :, part] = full
                xh[rows_of(f), part], xl[rows_of(f), part] = halves(full)
                ends.append(full)
            return ends

        for f in range(FIELDS):
            ends = complete(f, outer)
            tr[0, f] = jnp.where(lane < 64, ends[0], ends[1])
        pack_pairs(lambda f: tr[0, f, 24:32, :], True, send_x.at[0])
        pack_pairs(lambda f: tr[0, f, 0:8, :], False, send_x.at[1])

        @pl.when(step == 0)
        def _():
            pl.semaphore_wait(barrier, arrivals)

        made = copies(step)

        def send(d):
            for k in (2 * d, 2 * d + 1):

                @pl.when(sending(k))
                def _(k=k):
                    made[k].start()

        send(0)
        last_order(inner)
        for f in range(FIELDS):
            complete(f, inner)
        faces = dot(xh[...], pick[...]) + dot(xl[...], pick[...])
        for f in range(FIELDS):
            tr[1, f] = faces[rows_of(f), 0:128]
            tr[2, f] = faces[rows_of(f), 128:256]
        for f in range(FIELDS):
            send_z[0, f] = pack_z(f, True)
            send_z[1, f] = pack_z(f, False)
        send(2)
        pack_pairs(lambda f: pack_rows_y(f, 6), True, send_y.at[0])
        pack_pairs(lambda f: pack_rows_y(f, 0), False, send_y.at[1])
        send(1)
        derive()
        for j in range(4):
            part = slice(128 * j, 128 * (j + 1))
            for f, rate in enumerate(rates(part)):
                acc[f, :, part] = q[f, :, part] + DT_STEP * rate

        def receive(d):
            for k in (2 * d, 2 * d + 1):

                @pl.when(receiving(k))
                def _(k=k):
                    made[k].wait_recv()

        receive(1)
        corrections(step, 1)
        receive(2)
        corrections(step, 2)
        spread[...] = dot(ch[...], lift[...]) + dot(cl[...], lift[...])
        for f in range(FIELDS):
            for j in range(4):
                part = slice(128 * j, 128 * (j + 1))
                full = acc[f, :, part] + (DT_STEP * LIFT_COEF) * spread[rows_of(f), part]
                if j in (1, 2):
                    q[f, :, part] = full
                    xh[rows_of(f), part], xl[rows_of(f), part] = halves(full)
                else:
                    acc[f, :, part] = full
        receive(0)
        corrections(step, 0)
        for f in range(FIELDS):
            for j, mine in ((0, lane < 64), (3, lane >= 64)):
                part = slice(128 * j, 128 * (j + 1))
                full = acc[f, :, part] + jnp.where(mine, (DT_STEP * LIFT_COEF) * cx[f], 0.0)
                q[f, :, part] = full
                xh[rows_of(f), part], xl[rows_of(f), part] = halves(full)
        for k in range(6):

            @pl.when(sending(k))
            def _(k=k):
                made[k].wait_send()

        return carry

    lax.fori_loop(0, STEPS, step_body, 0)


def shards(
    wavefield, deriv_ops, density, lame_first, shear_modulus, high_order, element_cell, face_orient
):
    wave = jnp.swapaxes(wavefield[0, 0, 0], 0, 1)
    row = (1, ELEMENTS)
    vmem = pl.BlockSpec(memory_space=pltpu.VMEM)
    any_space = pl.BlockSpec(memory_space=pltpu.HBM)
    field = (FIELDS, ELEMENTS, NODES)
    total = FIELDS * ELEMENTS
    state = pl.pallas_call(
        kernel,
        out_shape=(
            jax.ShapeDtypeStruct(field, F32),
            jax.ShapeDtypeStruct((ELEMENTS, 3 * ELEMENTS), F32),
        ),
        in_specs=[any_space] * 8,
        out_specs=(vmem, vmem),
        scratch_shapes=[
            pltpu.VMEM(field, F32),
            pltpu.VMEM(row, F32),
            pltpu.VMEM(row, F32),
            pltpu.VMEM(row, F32),
            pltpu.VMEM(row, I32),
            pltpu.VMEM(row, I32),
            pltpu.VMEM((6, 1, ELEMENTS), I32),
            pltpu.VMEM((3, NODES, NODES), F32),
            pltpu.VMEM((3, NODES, NODES), BF16),
            pltpu.VMEM((3, NODES, NODES), BF16),
            pltpu.VMEM((16, ELEMENTS), F32),
            pltpu.VMEM((4, ELEMENTS, 128), F32),
            pltpu.VMEM((3, ELEMENTS, 128), I32),
            pltpu.VMEM(field, F32),
            pltpu.VMEM((total, NODES), BF16),
            pltpu.VMEM((total, NODES), BF16),
            pltpu.VMEM((3, 6 * ELEMENTS, NODES), F32),
            pltpu.VMEM((NODES, 256), BF16),
            pltpu.VMEM((256, NODES), BF16),
            pltpu.VMEM((3, FIELDS, ELEMENTS, 128), F32),
            pltpu.VMEM((total, 256), BF16),
            pltpu.VMEM((total, 256), BF16),
            pltpu.VMEM((FIELDS, ELEMENTS, 128), F32),
            pltpu.VMEM((total, NODES), F32),
            pltpu.VMEM((ELEMENTS, 2 * HOT), BF16),
            pltpu.VMEM((3, HOT, 128), F32),
            pltpu.VMEM((FIELDS, HOT, NODES), F32),
            pltpu.VMEM((FIELDS * HOT, NODES), BF16),
            pltpu.VMEM((FIELDS * HOT, NODES), BF16),
            pltpu.VMEM((3, 6 * HOT, NODES), F32),
            pltpu.VMEM((HOT, ELEMENTS), BF16),
            pltpu.VMEM((2, 5, 8, 128), F32),
            pltpu.VMEM((2, 5, 8, 128), F32),
            pltpu.VMEM((2, FIELDS, 8, 128), F32),
            pltpu.VMEM((STEPS, 2, 5, 8, 128), F32),
            pltpu.VMEM((STEPS, 2, 5, 8, 128), F32),
            pltpu.VMEM((STEPS, 2, FIELDS, 8, 128), F32),
            pltpu.SemaphoreType.DMA((FIELDS,)),
            pltpu.SemaphoreType.DMA((3,)),
            pltpu.SemaphoreType.DMA((STEPS, 6)),
            pltpu.SemaphoreType.DMA((STEPS, 6)),
        ],
        compiler_params=pltpu.CompilerParams(
            collective_id=0, has_side_effects=True, vmem_limit_bytes=24 * 1024 * 1024
        ),
        name="elastic_steps",
    )(
        *(
            pltpu.with_memory_space_constraint(x, pltpu.HBM)
            for x in (
                wave,
                deriv_ops,
                density.reshape(row),
                lame_first.reshape(row),
                shear_modulus.reshape(row),
                high_order.reshape(row),
                element_cell.reshape(row),
                face_orient.reshape(6, 1, ELEMENTS),
            )
        ),
    )
    result = pl.pallas_call(
        restore,
        out_shape=jax.ShapeDtypeStruct(field, F32),
        in_specs=[vmem, vmem],
        out_specs=any_space,
        scratch_shapes=[pltpu.VMEM(field, F32), pltpu.SemaphoreType.DMA((FIELDS,))],
        compiler_params=pltpu.CompilerParams(vmem_limit_bytes=8 * 1024 * 1024),
        name="restore",
    )(*state)
    return jnp.swapaxes(result, 0, 1)[None, None, None]


def solution(mesh):
    row = P("gx", "gy", "ha", None)
    whole = P("gx", "gy", "ha", None, None, None)
    return jax.shard_map(
        shards,
        mesh=mesh,
        in_specs=(whole, P(), row, row, row, row, row, P("gx", "gy", "ha", None, None)),
        out_specs=whole,
        check_vma=False,
    )
```

```python
import math

import jax
import jax.numpy as jnp
from jax import lax
from jax.experimental import pallas as pl
from jax.experimental.pallas import tpu as pltpu
from jax.sharding import PartitionSpec as P

ELEMENTS = 32
HOT = 16
FIELDS = 9
NODES = 512
STEPS = 2
DT_STEP = 0.8
LIFT_COEF = 2.0
X_FIELDS = (0, 1, 2, 3, 6, 8)
Y_FIELDS = (0, 1, 2, 6, 4, 7)
Z_FIELDS = (0, 1, 2, 8, 7, 5)
AXIS_FIELDS = (X_FIELDS, Y_FIELDS, Z_FIELDS)
MESH_AXES = ("gx", "gy", "ha")
SERIES = tuple(DT_STEP**k / math.factorial(k + 1) for k in range(6))
F32 = jnp.float32
BF16 = jnp.bfloat16
I32 = jnp.int32
NT = (((1,), (1,)), ((), ()))
HIGHEST = lax.Precision.HIGHEST


def dot(a, b):
    return jnp.dot(a, b, preferred_element_type=F32)


def halves(value):
    high = value.astype(BF16)
    return high, (value - high.astype(F32)).astype(BF16)


def thirds(value):
    high = value.astype(BF16)
    rest = value - high.astype(F32)
    mid = rest.astype(BF16)
    return high, mid, (rest - mid.astype(F32)).astype(BF16)


def rows_of(field):
    return slice(ELEMENTS * field, ELEMENTS * (field + 1))


def iota(shape, dim):
    return lax.broadcasted_iota(I32, shape, dim)


def face_node(column):
    face = column // 64
    p = (column // 8) % 8
    r = column % 8
    far = 7 * (face % 2)
    return jnp.where(face < 2, p * 64 + far * 8 + r, p * 64 + r * 8 + far)


def restore(state, gather, out, full, sems):
    stores = [pltpu.make_async_copy(full.at[f], out.at[f], sems.at[f]) for f in range(FIELDS)]
    gather_out = gather[...].astype(BF16)
    for f in range(FIELDS):
        full[f] = dot(gather_out, jnp.concatenate(thirds(state[f]), axis=0))
        stores[f].start()
    for store in stores:
        store.wait()


def kernel(
    wave_in, dops, dens_in, lame_in, shear_in, hot_in, cell_in, orient_in, q, gather_out,
    wave, dens, lame, shear, hot, cell, orient,
    wf, wh, wl, small, coef, index, acc, xh, xl, deriv, pick, lift, tr, ch, cl, cx, spread,
    hot_in_rows, hot_coef, hot_sum, yh, yl, hot_deriv, hot_sel,
    send_x, send_y, send_z, recv_x, recv_y, recv_z, small_sem, load_sem, send_sem, recv_sem,
):
    barrier = pltpu.get_barrier_semaphore()
    place = [lax.axis_index(a) for a in MESH_AXES]
    count = [lax.axis_size(a) for a in MESH_AXES]
    up = [{a: lax.rem(i + 1, n)} for a, i, n in zip(MESH_AXES, place, count)]
    down = [{a: lax.rem(i + n - 1, n)} for a, i, n in zip(MESH_AXES, place, count)]
    small_loads = [
        pltpu.make_async_copy(source, dest, small_sem.at[i])
        for i, (source, dest) in enumerate(
            (
                (cell_in, cell), (hot_in, hot), (dens_in, dens), (lame_in, lame),
                (shear_in, shear), (orient_in, orient), (wave_in, wave),
            )
        )
    ]
    for load in small_loads:
        load.start()
    loads = [pltpu.make_async_copy(dops.at[a], wf.at[a], load_sem.at[a]) for a in range(3)]
    for load in loads:
        load.start()

    arrivals = 0
    for d in range(3):
        for target, steps_left in ((up[d], count[d] - 1 - place[d]), (down[d], place[d])):

            @pl.when(steps_left > 0)
            def _(target=target):
                pl.semaphore_signal(barrier, 1, device_id=target, device_id_type=pl.DeviceIdType.MESH)

            arrivals = arrivals + lax.div(steps_left + count[d] - 1, count[d])

    pick[...] = (iota((NODES, 256), 0) == face_node(iota((NODES, 256), 1))).astype(BF16)
    lift[...] = (iota((256, NODES), 1) == face_node(iota((256, NODES), 0))).astype(BF16)

    for recv, at, n in zip((recv_x, recv_y, recv_z), place, count):
        for edge, slot in ((0, 0), (n - 1, 1)):

            @pl.when(at == edge)
            def _(recv=recv, slot=slot):
                for s in range(STEPS):
                    recv[s, slot] = jnp.zeros_like(recv[s, slot])

    def derive():
        for a, fields in enumerate(AXIS_FIELDS):
            h = jnp.concatenate([xh[rows_of(f), :] for f in fields], axis=0)
            l = jnp.concatenate([xl[rows_of(f), :] for f in fields], axis=0)
            deriv[a] = dot(h, wh[a]) + dot(l, wh[a]) + dot(h, wl[a])

    small[...] = jnp.zeros_like(small)
    for load in small_loads[:-1]:
        load.wait()
    small[0:1, :] = dens[...]
    small[1:2, :] = lame[...]
    small[2:3, :] = shear[...]
    small[3:4, :] = hot[...].astype(F32)
    for i in range(6):
        small[4 + i : 5 + i, :] = orient[i].astype(F32)
    small[10:11, :] = cell[...].astype(F32)
    square = (ELEMENTS, ELEMENTS)
    place_cell = (iota(square, 0) == jnp.broadcast_to(cell[...], square)).astype(F32)
    same = (iota(square, 0) == iota(square, 1)).astype(BF16)
    cell_row = jnp.broadcast_to(cell[...], (8, ELEMENTS)).astype(F32).astype(BF16)
    cell_col = lax.dot_general(same, cell_row, NT, preferred_element_type=F32)[:, 0:1]
    triple = (ELEMENTS, 3 * ELEMENTS)
    gather_out[...] = (cell_col.astype(I32) == iota(triple, 1) % ELEMENTS).astype(F32)
    by_cell = lax.dot_general(place_cell, small[...], NT, precision=HIGHEST)
    wide = (ELEMENTS, 128)
    inv_rho = 1.0 / by_cell[:, 0:1]
    lame_col = by_cell[:, 1:2]
    shear_col = by_cell[:, 2:3]
    coef[0] = jnp.broadcast_to(inv_rho, wide)
    coef[1] = jnp.broadcast_to(lame_col, wide)
    coef[2] = jnp.broadcast_to(shear_col, wide)
    coef[3] = jnp.broadcast_to(jnp.sqrt((lame_col + 2.0 * shear_col) * inv_rho), wide)
    lane = iota(wide, 1)
    p_pos = (lane // 8) % 8
    r_pos = lane % 8
    for d in range(3):
        low = jnp.broadcast_to(by_cell[:, 4 + 2 * d : 5 + 2 * d], wide)
        high = jnp.broadcast_to(by_cell[:, 5 + 2 * d : 6 + 2 * d], wide)
        code = jnp.where(lane < 64, low, high).astype(I32)
        p_src = jnp.where((code & 1) != 0, 7 - p_pos, p_pos)
        r_src = jnp.where((code & 2) != 0, 7 - r_pos, r_pos)
        node = jnp.where((code & 4) != 0, r_src * 8 + p_src, p_src * 8 + r_src)
        index[d] = node + jnp.where(lane < 64, 64, 0)
    slots = (HOT, ELEMENTS)
    flag_row = lax.dot_general(small[...], place_cell, NT, precision=HIGHEST)[3:4, :]
    upto = (iota(square, 0) <= iota(square, 1)).astype(F32)
    rank_row = lax.dot_general(
        jnp.broadcast_to(flag_row, (8, ELEMENTS)), upto, (((1,), (0,)), ((), ())), precision=HIGHEST
    )[0:1, :].astype(I32)
    chosen = (iota(slots, 0) + 1 == jnp.broadcast_to(rank_row, slots)) & (
        jnp.broadcast_to(flag_row, slots) > 0.5
    )
    select = chosen.astype(F32)
    hot_sel[...] = select.astype(BF16)
    of_slot = lax.dot_general(select, by_cell, (((1,), (0,)), ((), ())), precision=HIGHEST)
    filled = of_slot[:, 0:1] > 0.0
    hot_coef[0] = jnp.broadcast_to(
        jnp.where(filled, 1.0 / jnp.where(filled, of_slot[:, 0:1], 1.0), 0.0), (HOT, 128)
    )
    hot_coef[1] = jnp.broadcast_to(of_slot[:, 1:2], (HOT, 128))
    hot_coef[2] = jnp.broadcast_to(of_slot[:, 2:3], (HOT, 128))
    slot_col = iota((ELEMENTS, 2 * HOT), 1) % HOT + 1
    below = (iota(square, 1) <= iota(square, 0)).astype(F32)
    rank_col = lax.dot_general(
        below, jnp.broadcast_to(by_cell[:, 3:4], (ELEMENTS, 8)), (((1,), (0,)), ((), ())), precision=HIGHEST
    )[:, 0:1]
    back = (slot_col == rank_col.astype(I32)) & (by_cell[:, 3:4] > 0.5)
    hot_in_rows[...] = back.astype(BF16)
    cells = jnp.concatenate([cell[...]] * 3, axis=1)
    gather_in = (iota(triple, 0) == jnp.broadcast_to(cells, triple)).astype(BF16)
    small_loads[-1].wait()
    for f in range(FIELDS):
        full = dot(gather_in, jnp.concatenate(thirds(wave[f]), axis=0))
        q[f] = full
        xh[rows_of(f), :], xl[rows_of(f), :] = halves(full)

    for a in range(3):
        loads[a].wait()

        def split(i, carry, a=a):
            part = pl.ds(pl.multiple_of(i * 64, 64), 64)
            h, l = halves(wf[a, part, :])
            wh[a, part, :] = h
            wl[a, part, :] = l
            return carry

        lax.fori_loop(0, NODES // 64, split, 0)

    def hot_rows(field):
        return slice(HOT * field, HOT * (field + 1))

    def derive_hot(parts=(slice(0, NODES),)):
        for a, fields in enumerate(AXIS_FIELDS):
            h = [yh[hot_rows(f), :] for f in fields]
            l = [yl[hot_rows(f), :] for f in fields]
            right = jnp.concatenate([wh[a, :, part] for part in parts], axis=1)
            both = dot(jnp.concatenate(h + l, axis=0), right)
            right = jnp.concatenate([wl[a, :, part] for part in parts], axis=1)
            cross = dot(jnp.concatenate(h, axis=0), right)
            total = both[0 : 6 * HOT] + (both[6 * HOT :] + cross)
            at = 0
            for part in parts:
                width = part.stop - part.start
                hot_deriv[a, :, part] = total[:, at : at + width]
                at += width

    def rates(part, source=deriv, rows=rows_of, factors=coef):
        x = [source[0, rows(i), part] for i in range(6)]
        y = [source[1, rows(i), part] for i in range(6)]
        z = [source[2, rows(i), part] for i in range(6)]
        inv, lam, mu = factors[0], factors[1], factors[2]
        lam_div = lam * (x[0] + y[1] + z[2])
        mu2 = 2.0 * mu
        return [
            inv * (x[3] + y[3] + z[3]),
            inv * (x[4] + y[4] + z[4]),
            inv * (x[5] + y[5] + z[5]),
            lam_div + mu2 * x[0],
            lam_div + mu2 * y[1],
            lam_div + mu2 * z[2],
            mu * (x[1] + y[0]),
            mu * (y[2] + z[1]),
            mu * (x[2] + z[0]),
        ]

    def advance(first, weight):
        derive()
        for j in range(4):
            part = slice(128 * j, 128 * (j + 1))
            for f, rate in enumerate(rates(part)):
                term = weight * rate
                base = q if first else acc
                acc[f, :, part] = base[f, :, part] + term
                xh[rows_of(f), part], xl[rows_of(f), part] = halves(rate)

    def pack_pairs(tile, upper, dest):
        keep = (iota((8, 128), 1) >= 64) if upper else (iota((8, 128), 1) < 64)
        for f in range(4):
            dest[f] = jnp.where(keep, tile(f), pltpu.roll(tile(f + 5), 64, 1))
        dest[4] = tile(4)

    def unpack_pairs(source, f):
        return source[f] if f < 5 else pltpu.roll(source[f - 5], 64, 1)

    sub = iota((8, 128), 0)
    lo_lane = iota((8, 128), 1) < 64
    even = sub % 2 == 0

    def pack_rows_y(f, first_row):
        result = None
        for a in range(4):
            tile = tr[1, f, 8 * a : 8 * a + 8, :]
            shift = (2 * a - first_row) % 8
            moved = pltpu.roll(tile, shift, 0) if shift else tile
            result = moved if a == 0 else jnp.where(sub // 2 == a, moved, result)
        return result

    def pack_z(f, odd):
        strips = []
        for a in range(2):
            one = tr[2, f, 8 * a : 8 * a + 8, :]
            two = tr[2, f, 8 * a + 16 : 8 * a + 24, :]
            if odd:
                strips.append(jnp.where(even, pltpu.roll(two, 7, 0), one))
            else:
                strips.append(jnp.where(even, one, pltpu.roll(two, 1, 0)))
        keep = jnp.logical_not(lo_lane) if odd else lo_lane
        return jnp.where(keep, strips[0], pltpu.roll(strips[1], 64, 1))

    sends = (send_x, send_y, send_z)
    recvs = (recv_x, recv_y, recv_z)

    def copies(step):
        made = []
        for d in range(3):
            for way, target in ((0, up[d]), (1, down[d])):
                made.append(
                    pltpu.make_async_remote_copy(
                        src_ref=sends[d].at[way],
                        dst_ref=recvs[d].at[step, way],
                        send_sem=send_sem.at[step, 2 * d + way],
                        recv_sem=recv_sem.at[step, 2 * d + way],
                        device_id=target,
                        device_id_type=pl.DeviceIdType.MESH,
                    )
                )
        return made

    def sending(k):
        d, way = divmod(k, 2)
        return place[d] < count[d] - 1 if way == 0 else place[d] > 0

    def receiving(k):
        d, way = divmod(k, 2)
        return place[d] > 0 if way == 0 else place[d] < count[d] - 1

    def neighbours(step, d, f, a):
        tile = tr[d, f, 8 * a : 8 * a + 8, :]
        if d == 0:
            before = unpack_pairs(recv_x.at[step, 0], f) if a == 0 else tr[0, f, 8 * a - 8 : 8 * a, :]
            after = unpack_pairs(recv_x.at[step, 1], f) if a == 3 else tr[0, f, 8 * a + 8 : 8 * a + 16, :]
        elif d == 1:
            low = unpack_pairs(recv_y.at[step, 0], f)
            low = pltpu.roll(low, (8 - 2 * a) % 8, 0) if a else low
            before = jnp.where(sub < 2, low, pltpu.roll(tile, 2, 0))
            high = unpack_pairs(recv_y.at[step, 1], f)
            high = pltpu.roll(high, (6 - 2 * a) % 8, 0) if a < 3 else high
            after = jnp.where(sub >= 6, high, pltpu.roll(tile, 6, 0))
        else:
            low = recv_z[step, 0, f]
            high = recv_z[step, 1, f]
            if a % 2:
                low = pltpu.roll(low, 64, 1)
                high = pltpu.roll(high, 64, 1)
            if a < 2:
                low = pltpu.roll(low, 7, 0)
                high = pltpu.roll(high, 1, 0)
            before = jnp.where(even, low, pltpu.roll(tile, 1, 0))
            after = jnp.where(even, pltpu.roll(tile, 7, 0), high)
        return jnp.where(lo_lane, after, before)

    def corrections(step, d):
        sign = jnp.where(lo_lane, -1.0, 1.0)
        for a in range(4):
            rows = slice(8 * a, 8 * a + 8)
            source = index[d, rows, :]
            w = [
                jnp.take_along_axis(neighbours(step, d, f, a), source, axis=1) - tr[d, f, rows, :]
                for f in range(FIELDS)
            ]
            inv, lam, mu, speed = [coef[i, rows, :] for i in range(4)]
            stiff = lam + 2.0 * mu
            if d == 0:
                lam_v = lam * w[0]
                flux = [inv * w[3], inv * w[6], inv * w[8], stiff * w[0], lam_v, lam_v,
                        mu * w[1], None, mu * w[2]]
            elif d == 1:
                lam_v = lam * w[1]
                flux = [inv * w[6], inv * w[4], inv * w[7], lam_v, stiff * w[1], lam_v,
                        mu * w[0], mu * w[2], None]
            else:
                lam_v = lam * w[2]
                flux = [inv * w[8], inv * w[7], inv * w[5], lam_v, lam_v, stiff * w[2],
                        None, mu * w[1], mu * w[0]]
            for f in range(FIELDS):
                fixed = speed * w[f]
                if flux[f] is not None:
                    fixed = fixed + sign * flux[f]
                fixed = 0.5 * fixed
                if d == 0:
                    cx[f, rows, :] = fixed
                else:
                    tr[d, f, rows, :] = fixed
        if d:
            part = slice(128 * (d - 1), 128 * d)
            for f in range(FIELDS):
                ch[rows_of(f), part], cl[rows_of(f), part] = halves(tr[d, f])

    def step_body(step, carry):
        advance(True, SERIES[1])
        advance(False, SERIES[2])
        for f in range(FIELDS):
            yh[hot_rows(f), :] = dot(hot_sel[...], xh[rows_of(f), :]).astype(BF16)
            yl[hot_rows(f), :] = dot(hot_sel[...], xl[rows_of(f), :]).astype(BF16)
            hot_sum[f] = jnp.zeros_like(hot_sum[f])

        def higher(k, c):
            weight = jnp.where(k == 0, SERIES[3], SERIES[4]).astype(F32)
            derive_hot()
            for j in range(4):
                part = slice(128 * j, 128 * (j + 1))
                for f, rate in enumerate(rates(part, hot_deriv, hot_rows, hot_coef)):
                    hot_sum[f, :, part] = hot_sum[f, :, part] + weight * rate
                    yh[hot_rows(f), part], yl[hot_rows(f), part] = halves(rate)
            return c

        @pl.when(step == 0)
        def _():
            pl.semaphore_wait(barrier, arrivals)

        lax.fori_loop(0, 2, higher, 0)

        def last_order(parts):
            derive_hot(parts)
            for part in parts:
                for f, rate in enumerate(rates(part, hot_deriv, hot_rows, hot_coef)):
                    hot_sum[f, :, part] = hot_sum[f, :, part] + SERIES[5] * rate

        outer = (slice(0, 128), slice(384, 512))
        inner = (slice(128, 256), slice(256, 384))
        last_order(outer)
        def complete(f, parts):
            extra = jnp.concatenate([hot_sum[f, :, part] for part in parts], axis=1)
            extra = dot(hot_in_rows[...], jnp.concatenate(halves(extra), axis=0))
            ends = []
            for i, part in enumerate(parts):
                full = acc[f, :, part] + extra[:, 128 * i : 128 * (i + 1)]
                acc[f, :, part] = full
                xh[rows_of(f), part], xl[rows_of(f), part] = halves(full)
                ends.append(full)
            return ends

        for f in range(FIELDS):
            ends = complete(f, outer)
            tr[0, f] = jnp.where(lane < 64, ends[0], ends[1])
        pack_pairs(lambda f: tr[0, f, 24:32, :], True, send_x.at[0])
        pack_pairs(lambda f: tr[0, f, 0:8, :], False, send_x.at[1])

        made = copies(step)

        def send(d):
            for k in (2 * d, 2 * d + 1):

                @pl.when(sending(k))
                def _(k=k):
                    made[k].start()

        send(0)
        last_order(inner)
        for f in range(FIELDS):
            complete(f, inner)
        faces = dot(xh[...], pick[...]) + dot(xl[...], pick[...])
        for f in range(FIELDS):
            tr[1, f] = faces[rows_of(f), 0:128]
            tr[2, f] = faces[rows_of(f), 128:256]
        for f in range(FIELDS):
            send_z[0, f] = pack_z(f, True)
            send_z[1, f] = pack_z(f, False)
        send(2)
        pack_pairs(lambda f: pack_rows_y(f, 6), True, send_y.at[0])
        pack_pairs(lambda f: pack_rows_y(f, 0), False, send_y.at[1])
        send(1)
        derive()
        for j in range(4):
            part = slice(128 * j, 128 * (j + 1))
            for f, rate in enumerate(rates(part)):
                acc[f, :, part] = q[f, :, part] + DT_STEP * rate

        def receive(d):
            for k in (2 * d, 2 * d + 1):

                @pl.when(receiving(k))
                def _(k=k):
                    made[k].wait_recv()

        receive(1)
        corrections(step, 1)
        receive(2)
        corrections(step, 2)
        spread[...] = dot(ch[...], lift[...]) + dot(cl[...], lift[...])
        for f in range(FIELDS):
            for j in range(4):
                part = slice(128 * j, 128 * (j + 1))
                full = acc[f, :, part] + (DT_STEP * LIFT_COEF) * spread[rows_of(f), part]
                if j in (1, 2):
                    q[f, :, part] = full
                    xh[rows_of(f), part], xl[rows_of(f), part] = halves(full)
                else:
                    acc[f, :, part] = full
        receive(0)
        corrections(step, 0)
        for f in range(FIELDS):
            for j, mine in ((0, lane < 64), (3, lane >= 64)):
                part = slice(128 * j, 128 * (j + 1))
                full = acc[f, :, part] + jnp.where(mine, (DT_STEP * LIFT_COEF) * cx[f], 0.0)
                q[f, :, part] = full
                xh[rows_of(f), part], xl[rows_of(f), part] = halves(full)
        for k in range(6):

            @pl.when(sending(k))
            def _(k=k):
                made[k].wait_send()

        return carry

    lax.fori_loop(0, STEPS, step_body, 0)


def shards(
    wavefield, deriv_ops, density, lame_first, shear_modulus, high_order, element_cell, face_orient
):
    wave = jnp.swapaxes(wavefield[0, 0, 0], 0, 1)
    row = (1, ELEMENTS)
    vmem = pl.BlockSpec(memory_space=pltpu.VMEM)
    any_space = pl.BlockSpec(memory_space=pltpu.HBM)
    field = (FIELDS, ELEMENTS, NODES)
    total = FIELDS * ELEMENTS
    state = pl.pallas_call(
        kernel,
        out_shape=(
            jax.ShapeDtypeStruct(field, F32),
            jax.ShapeDtypeStruct((ELEMENTS, 3 * ELEMENTS), F32),
        ),
        in_specs=[any_space] * 8,
        out_specs=(vmem, vmem),
        scratch_shapes=[
            pltpu.VMEM(field, F32),
            pltpu.VMEM(row, F32),
            pltpu.VMEM(row, F32),
            pltpu.VMEM(row, F32),
            pltpu.VMEM(row, I32),
            pltpu.VMEM(row, I32),
            pltpu.VMEM((6, 1, ELEMENTS), I32),
            pltpu.VMEM((3, NODES, NODES), F32),
            pltpu.VMEM((3, NODES, NODES), BF16),
            pltpu.VMEM((3, NODES, NODES), BF16),
            pltpu.VMEM((16, ELEMENTS), F32),
            pltpu.VMEM((4, ELEMENTS, 128), F32),
            pltpu.VMEM((3, ELEMENTS, 128), I32),
            pltpu.VMEM(field, F32),
            pltpu.VMEM((total, NODES), BF16),
            pltpu.VMEM((total, NODES), BF16),
            pltpu.VMEM((3, 6 * ELEMENTS, NODES), F32),
            pltpu.VMEM((NODES, 256), BF16),
            pltpu.VMEM((256, NODES), BF16),
            pltpu.VMEM((3, FIELDS, ELEMENTS, 128), F32),
            pltpu.VMEM((total, 256), BF16),
            pltpu.VMEM((total, 256), BF16),
            pltpu.VMEM((FIELDS, ELEMENTS, 128), F32),
            pltpu.VMEM((total, NODES), F32),
            pltpu.VMEM((ELEMENTS, 2 * HOT), BF16),
            pltpu.VMEM((3, HOT, 128), F32),
            pltpu.VMEM((FIELDS, HOT, NODES), F32),
            pltpu.VMEM((FIELDS * HOT, NODES), BF16),
            pltpu.VMEM((FIELDS * HOT, NODES), BF16),
            pltpu.VMEM((3, 6 * HOT, NODES), F32),
            pltpu.VMEM((HOT, ELEMENTS), BF16),
            pltpu.VMEM((2, 5, 8, 128), F32),
            pltpu.VMEM((2, 5, 8, 128), F32),
            pltpu.VMEM((2, FIELDS, 8, 128), F32),
            pltpu.VMEM((STEPS, 2, 5, 8, 128), F32),
            pltpu.VMEM((STEPS, 2, 5, 8, 128), F32),
            pltpu.VMEM((STEPS, 2, FIELDS, 8, 128), F32),
            pltpu.SemaphoreType.DMA((FIELDS,)),
            pltpu.SemaphoreType.DMA((3,)),
            pltpu.SemaphoreType.DMA((STEPS, 6)),
            pltpu.SemaphoreType.DMA((STEPS, 6)),
        ],
        compiler_params=pltpu.CompilerParams(
            collective_id=0, has_side_effects=True, vmem_limit_bytes=24 * 1024 * 1024
        ),
        name="elastic_steps",
    )(
        *(
            pltpu.with_memory_space_constraint(x, pltpu.HBM)
            for x in (
                wave,
                deriv_ops,
                density.reshape(row),
                lame_first.reshape(row),
                shear_modulus.reshape(row),
                high_order.reshape(row),
                element_cell.reshape(row),
                face_orient.reshape(6, 1, ELEMENTS),
            )
        ),
    )
    result = pl.pallas_call(
        restore,
        out_shape=jax.ShapeDtypeStruct(field, F32),
        in_specs=[vmem, vmem],
        out_specs=any_space,
        scratch_shapes=[pltpu.VMEM(field, F32), pltpu.SemaphoreType.DMA((FIELDS,))],
        compiler_params=pltpu.CompilerParams(vmem_limit_bytes=8 * 1024 * 1024),
        name="restore",
    )(*state)
    return jnp.swapaxes(result, 0, 1)[None, None, None]


def solution(mesh):
    row = P("gx", "gy", "ha", None)
    whole = P("gx", "gy", "ha", None, None, None)
    return jax.shard_map(
        shards,
        mesh=mesh,
        in_specs=(whole, P(), row, row, row, row, row, P("gx", "gy", "ha", None, None)),
        out_specs=whole,
        check_vma=False,
    )
```
